32 devices in a mesh: patch: 2 (over y), sky: 4 (over z), exp: 2 (over core), band: 2 (over x).
Axes of the slice: x: 2, y: 2, z: 4, core: 2. Of those that a mesh axis runs over, the one named last changes fastest.
Arguments:
- images: bfloat16 [2, 20, 1024, 512], P('band', 'exp', ('patch', 'sky')), parts along dimension 2, may hold values from -400 to 400
- valid_mask: int32 [2, 20, 1024, 512], P('band', 'exp', ('patch', 'sky')), parts along dimension 2, may hold values from 0 to 1, as said below
- row_kernel: float32 [2, 20, 31], P('band', 'exp'), may hold values from 0.01 to 0.06
- col_kernel: float32 [2, 20, 31], P('band', 'exp'), may hold values from 0.01 to 0.06
- exp_group: int32 [2, 20], P('band', 'exp'), may hold values from 0 to 15
- zero_point: float32 [2, 16], P('band'), may hold values from 0.5 to 2
- psf_row: float32 [2, 31], P('band'), may hold values from 0.01 to 0.06
- psf_col: float32 [2, 31], P('band'), may hold values from 0.01 to 0.06
Outputs:
- coadd_image: float32 [2, 1024, 512], P('band', ('patch', 'sky')), parts along dimension 1
- detection: float32 [1024, 512], P(('patch', 'sky'), 'band'), parts along dimension 0
The draws below stay inside these ranges and needn't reach their ends.
There are 2 independent parts, one for each index of `patch`. The reference program is written for one: setup_inputs(seed, part) draws one part's arguments, and reference() takes and returns one part's arrays. A program takes and returns all parts, laid end to end along the dimension named above; an argument that names none is the same for every part. Nothing has to cross between parts.
Inputs may be any that keep to these rules, and one draw needn't show every extreme that they name: For every band and pixel at least 10 of the 20 visits have valid_mask 1; exactly that many at some pixels, all of them at others.
All inputs are finite; a program needn't handle non-finite values.
Results may differ from the reference program's by a relative error of at most 0.0006.
Values may be sent and summed in bfloat16 or wider, within the bound.
A program may use at most 64 MiB of HBM per device.

```python
import math
import jax
import jax.numpy as jnp
from jax import lax

COLS = 512
HALF = 15
REJECT = 4
GROUPS = 16
TAPS = 31
BANDS = 2
VIS_BAND = 20
ROWS = 512


def draw_images(key, part):
    key_noise, key_col, key_spike, key_sign = jax.random.split(key, 4)
    shape_all = (BANDS, VIS_BAND, ROWS, COLS)
    row_frac = jnp.arange(ROWS, dtype=jnp.float32) / max(ROWS - 1, 1)
    col_scale = 10.0 ** (jax.random.uniform(key_col, (COLS,), jnp.float32) - 0.5)
    jitter = jax.random.normal(key_noise, shape_all, jnp.float32)
    jitter = jnp.clip(jitter, -6.0, 6.0)
    row_scale = 10.0 ** (row_frac - 0.5)
    spike_on = (jax.random.randint(key_spike, shape_all, 0, 25) == 0).astype(jnp.float32)
    spike_sign = (jax.random.randint(key_sign, shape_all, 0, 2) * 2 - 1).astype(jnp.float32)
    sampled = (jitter + 12.0 * spike_on * spike_sign) * row_scale[:, None] * col_scale[None, :]
    return sampled.astype(jnp.bfloat16)


def draw_valid_mask(key, part):
    key_score, key_limit = jax.random.split(jax.random.fold_in(key, 7), 2)
    shape_all = (BANDS, VIS_BAND, ROWS, COLS)
    scores = jax.random.randint(key_score, shape_all, 0, 1 << 20) * VIS_BAND + jnp.arange(VIS_BAND, dtype=jnp.int32)[None, :, None, None]

    def count_below(visit_num, rank_count):
        picked = lax.dynamic_index_in_dim(scores, visit_num, 1, keepdims=True)
        return rank_count + (picked < scores).astype(jnp.int32)
    rank_count = lax.fori_loop(0, VIS_BAND, count_below, jnp.zeros(shape_all, jnp.int32))
    cutoff = jax.random.randint(key_limit, (BANDS, 1, ROWS, COLS), 2 * REJECT + 2, VIS_BAND + 1)
    return (rank_count < cutoff).astype(jnp.int32)


def touch_ends(drawn, key, low, largest):
    extent = drawn.shape
    index_at = [jax.random.randint(jax.random.fold_in(key, axis), (), 0, extent[axis]) for axis in range(len(extent))]
    drawn = drawn.at[tuple(index_at)].set(low)
    longest = extent.index(max(extent))
    index_at[longest] = (index_at[longest] + 1) % extent[longest]
    return drawn.at[tuple(index_at)].set(largest)


def steps_of(key, dims, pieces, smallest, high):
    factor_of, own = 1.0, jax.random.fold_in(key, 6)
    for dim, shards_of in pieces:
        heights = jnp.exp(jax.random.uniform(jax.random.fold_in(own, dim), (shards_of,), jnp.float32, smallest / len(pieces), high / len(pieces)))
        factor_of = factor_of * jnp.repeat(heights, dims[dim] // shards_of).reshape([-1 if axis == dim else 1 for axis in range(len(dims))])
    return factor_of


def setup_inputs(seed: int = 0, part: int = 0) -> dict:
    seeds = jax.random.split(jax.random.key(seed), 9)
    own_keys = jax.random.split(jax.random.fold_in(seeds[8], part), 9)
    images = draw_images(jax.random.fold_in(jax.random.fold_in(seeds[8], part), 71), part)
    valid_mask = draw_valid_mask(jax.random.fold_in(jax.random.fold_in(seeds[8], part), 71), part)
    row_kernel = jnp.clip(jnp.exp(math.log(0.06) - 1.7917595 * jax.random.uniform(seeds[2], (BANDS, VIS_BAND, TAPS), jnp.float32) ** steps_of(seeds[2], (BANDS, VIS_BAND, TAPS), ((0, 2), (1, 2)), -0.2, 0.2)), 0.01, 0.06)
    col_kernel = jnp.clip(jnp.exp(math.log(0.06) - 1.7917595 * jax.random.uniform(seeds[3], (BANDS, VIS_BAND, TAPS), jnp.float32) ** steps_of(seeds[3], (BANDS, VIS_BAND, TAPS), ((0, 2), (1, 2)), -0.2, 0.2)), 0.01, 0.06)
    exp_group = touch_ends(jax.random.randint(seeds[4], (BANDS, VIS_BAND), 0, GROUPS), jax.random.fold_in(seeds[4], 1), 0, GROUPS - 1).astype(jnp.int32)
    zero_point = jnp.clip(jnp.exp(math.log(2.0) - 1.3862944 * jax.random.uniform(seeds[5], (BANDS, GROUPS), jnp.float32) ** steps_of(seeds[5], (BANDS, GROUPS), ((0, 2),), -0.2, 0.2)), 0.5, 2.0)
    psf_row = jnp.clip(jnp.exp(math.log(0.06) - 1.7917595 * jax.random.uniform(seeds[6], (BANDS, TAPS), jnp.float32) ** steps_of(seeds[6], (BANDS, TAPS), ((0, 2),), -0.2, 0.2)), 0.01, 0.06)
    psf_col = jnp.clip(jnp.exp(math.log(0.06) - 1.7917595 * jax.random.uniform(seeds[7], (BANDS, TAPS), jnp.float32) ** steps_of(seeds[7], (BANDS, TAPS), ((0, 2),), -0.2, 0.2)), 0.01, 0.06)
    return dict(images=images, valid_mask=valid_mask, row_kernel=row_kernel, col_kernel=col_kernel, exp_group=exp_group, zero_point=zero_point, psf_row=psf_row, psf_col=psf_col)


SENTINEL = 1.0e30
EPSILON = 1.0e-5


def rows_filter(padded, kernel, height):
    result = kernel[..., 0][..., None, None] * padded[..., 0:height, :]
    for offset in range(1, TAPS):
        result = result + kernel[..., offset][..., None, None] * padded[..., offset:offset + height, :]
    return result


def cols_filter(grid_in, kernel):
    columns = grid_in.shape[-1]
    widths = [(0, 0)] * (grid_in.ndim - 1) + [(HALF, HALF)]
    padded = jnp.pad(grid_in, widths)
    result = kernel[..., 0][..., None, None] * padded[..., 0:columns]
    for offset in range(1, TAPS):
        result = result + kernel[..., offset][..., None, None] * padded[..., offset:offset + columns]
    return result


def one_band(inputs):
    band_images, band_valid, band_rows, band_cols, band_groups, band_points = inputs
    padded = jnp.pad(band_images.astype(jnp.float32), ((0, 0), (HALF, HALF), (0, 0)))
    smeared = cols_filter(rows_filter(padded, band_rows, ROWS), band_cols)
    matches = band_groups[:, None] == jnp.arange(GROUPS, dtype=jnp.int32)[None, :]
    flux_scale = jnp.sum(jnp.where(matches, band_points[None, :], jnp.float32(0.0)), axis=1)
    scaled_visits = flux_scale[:, None, None] * smeared
    usable = band_valid == 1
    upper_sum = jnp.sum(jnp.sort(jnp.where(usable, scaled_visits, -SENTINEL), axis=0)[VIS_BAND - REJECT:], axis=0)
    lower_sum = jnp.sum(jnp.sort(jnp.where(usable, scaled_visits, SENTINEL), axis=0)[:REJECT], axis=0)
    flux_sum = jnp.sum(jnp.where(usable, scaled_visits, jnp.float32(0.0)), axis=0)
    valid_count = jnp.sum(usable.astype(jnp.float32), axis=0)
    return (flux_sum - upper_sum - lower_sum) / (valid_count - 2 * REJECT)


def reference(images, valid_mask, row_kernel, col_kernel, exp_group, zero_point, psf_row, psf_col):
    coadd_image = lax.map(one_band, (images, valid_mask, row_kernel, col_kernel, exp_group, zero_point))
    padded = jnp.pad(coadd_image, ((0, 0), (HALF, HALF), (0, 0)))
    filtered = cols_filter(rows_filter(padded, psf_row, ROWS), psf_col)
    energy = filtered * filtered
    variance = jnp.sum(energy, axis=(1, 2)) / (ROWS * COLS) + EPSILON
    detection = jnp.sum(energy / variance[:, None, None], axis=0)
    return (coadd_image, detection)
```

```python
import functools

import jax
import jax.numpy as jnp
from jax import lax
from jax.experimental import pallas as pl
from jax.experimental.pallas import tpu as pltpu
from jax.sharding import PartitionSpec as P

MESH = pl.DeviceIdType.MESH
HALF = 15
REJECT = 4
TAPS = 31
SENTINEL = 1e30
EPSILON = 1e-05
PAD = 16
TILE = 128
HALVES = 2
BF = jnp.bfloat16
F32 = jnp.float32


def parts(value):
    high = value.astype(BF)
    return high, (value - high.astype(F32)).astype(BF)


def mm(a, b):
    return jnp.dot(a, b, preferred_element_type=F32)


def cols_filter(value, wh, wl):
    columns = value.shape[1]
    rows = value.shape[0]
    high, low = parts(value)
    windows = columns // TILE - 1

    def stack(part):
        return jnp.concatenate([part[:, n * TILE:(n + 2) * TILE] for n in range(windows)], axis=0)

    highs, lows = stack(high), stack(low)
    result = mm(highs, wh) + mm(lows, wh) + mm(highs, wl)
    seen = [result[n * rows:(n + 1) * rows] for n in range(windows)]
    left = lax.broadcasted_iota(jnp.int32, (rows, TILE), 1) < TILE // 2
    outs = [seen[0][:, 0:TILE]]
    for n in range(1, windows):
        outs.append(jnp.where(left, seen[n - 1][:, TILE:], seen[n][:, 0:TILE]))
    outs.append(seen[-1][:, TILE:])
    return outs


def swap(a, b):
    return jnp.minimum(a, b), jnp.maximum(a, b)


def sort4(a, b, c, d):
    a, b = swap(a, b)
    c, d = swap(c, d)
    a, c = swap(a, c)
    b, d = swap(b, d)
    b, c = swap(b, c)
    return [a, b, c, d]


def resort4(a, b, c, d):
    a, c = swap(a, c)
    b, d = swap(b, d)
    a, b = swap(a, b)
    c, d = swap(c, d)
    return [a, b, c, d]


def kernel(
    n_sky, n_band,
    img, mask, rk_in, ck_in, pr_in, pc_in, eg_in, zp_in,
    coadd_out, det_out,
    rk, ck, pr, pc, eg, zp, x, msk, taps, trow, tbnd, wh, wl, vals, cpad, energy, land, sums, det,
    arg_sem, img_sem, mask_sem, tap_send, tap_recv, far_send, far_recv, fmask_send, fmask_recv,
    halo_send, halo_recv, share_send, share_recv, co_send, co_recv, sum_send, sum_recv, en_send, en_recv, out_sem,
):
    visits, height, columns = img.shape[1:]
    mine = height // HALVES
    main = mine - PAD
    frame = mine + 2 * PAD
    kmain, kbnd = main + 2 * PAD, 3 * PAD
    width = columns // n_band
    chunks = visits // 2
    sky, band, exp = lax.axis_index("sky"), lax.axis_index("band"), lax.axis_index("exp")
    has_before, has_after = sky > 0, sky < n_sky - 1
    has_halo = jnp.where(exp == 0, sky, n_sky - 1 - sky) > 0
    n_peer = n_sky * n_band * HALVES
    me = (sky * n_band + band) * HALVES + exp

    def peer_of(step):
        peer = lax.rem(me + step, n_peer)
        chip = peer // HALVES
        return {"sky": chip // n_band, "band": lax.rem(chip, n_band), "exp": lax.rem(peer, HALVES)}

    other_core = {"exp": 1 - exp}

    def remote(source, target, send, recv, device):
        return pltpu.make_async_remote_copy(
            src_ref=source, dst_ref=target, send_sem=send, recv_sem=recv, device_id=device, device_id_type=MESH,
        )

    def al(value):
        return pl.multiple_of(value, PAD)

    small = [
        pltpu.make_async_copy(source, target, arg_sem.at[k])
        for k, (source, target) in enumerate(
            ((eg_in, eg), (zp_in, zp), (ck_in, ck), (pc_in, pc), (rk_in, rk), (pr_in, pr))
        )
    ]
    for copy in small:
        copy.start()

    barrier = pltpu.get_barrier_semaphore()

    def greet(step, carry):
        pl.semaphore_signal(barrier, inc=1, device_id=peer_of(step), device_id_type=MESH)
        return carry

    lax.fori_loop(1, n_peer, greet, 0)

    load_img = pltpu.make_async_copy(
        img.at[0, :, pl.ds(al(exp * (mine - PAD)), kmain), :],
        x.at[pl.ds(0, visits), pl.ds(al((1 - exp) * PAD), kmain), :], img_sem,
    )
    load_img.start()
    load_mask = pltpu.make_async_copy(
        mask.at[0, :, pl.ds(al(exp * mine), mine), :], msk.at[pl.ds(0, visits)], mask_sem
    )
    load_mask.start()
    pl.semaphore_wait(barrier, n_peer - 1)

    def halo(side, c):
        start, land_at = ((height - PAD, 0), (0, PAD + mine))[side]
        slot = jnp.where(exp == side, 0, visits) + c * 2
        return remote(
            img.at[0, pl.ds(c * 2, 2), pl.ds(start, PAD), :],
            x.at[pl.ds(slot, 2), pl.ds(land_at, PAD), :],
            halo_send.at[side, c], halo_recv.at[jnp.where(exp == side, 0, 1), c],
            {"sky": lax.rem(sky + (1, n_sky - 1)[side], n_sky), "exp": side},
        )

    def start_halo(c, carry):
        @pl.when(has_after)
        def _():
            halo(0, c).start()

        @pl.when(has_before)
        def _():
            halo(1, c).start()
        return carry

    lax.fori_loop(0, chunks, start_halo, 0)

    send_far = remote(
        img.at[0, :, pl.ds(al((1 - exp) * (mine - PAD)), kmain), :],
        x.at[pl.ds(visits, visits), pl.ds(al(exp * PAD), kmain), :],
        far_send, far_recv, other_core,
    )
    send_far.start()
    send_fmask = remote(
        mask.at[0, :, pl.ds(al((1 - exp) * mine), mine), :], msk.at[pl.ds(visits, visits)],
        fmask_send, fmask_recv, other_core,
    )
    send_fmask.start()

    taps[0] = jnp.zeros(taps.shape[1:], F32)
    for copy in small:
        copy.wait()
    for v in range(visits):
        taps[0, 0, v:v + 1, 0:TAPS] = rk[v]
    taps[0, 0, visits:visits + 1, 0:TAPS] = pr[...]
    for v in range(visits):
        taps[0, 1, v:v + 1, 0:TAPS] = ck[v] * zp[0, eg[0, v]]
    taps[0, 1, visits:visits + 1, 0:TAPS] = pc[...]
    at_row = lax.broadcasted_iota(jnp.int32, (TILE, TILE), 0)
    at_col = lax.broadcasted_iota(jnp.int32, (TILE, TILE), 1)
    flip = (at_col == lax.rem(HALF - at_row + TILE, TILE)).astype(F32)
    taps[0, 1] = jnp.dot(taps[0, 1], flip, preferred_element_type=F32, precision=lax.Precision.HIGHEST)
    send_taps = remote(taps.at[0], taps.at[1], tap_send, tap_recv, other_core)
    send_taps.start()

    @pl.when(jnp.logical_not(has_halo))
    def _():
        x[:, pl.ds(al(exp * (PAD + mine)), PAD), :] = jnp.zeros((HALVES * visits, PAD, columns), BF)
        cpad[pl.ds(al(exp * (PAD + height)), PAD), :] = jnp.zeros((PAD, columns), F32)

    before = at_row - at_col > TILE // 2
    after = at_col - at_row > TILE // 2

    def build(origin, v, slot):
        band_r = jnp.broadcast_to(taps[origin, 0, pl.ds(v, 1), :], (main, TILE))
        high, low = parts(pltpu.roll(band_r, 1, 1, stride=1, stride_axis=0))
        trow[slot, 0:main, :] = high
        trow[slot, main:, :] = low
        tbnd[slot, 0:PAD, :] = high[0:PAD]
        tbnd[slot, PAD:, :] = low[0:PAD]
        band_c = jnp.broadcast_to(taps[origin, 1, pl.ds(v, 1), :], (TILE, TILE))
        band_c = pltpu.roll(band_c, 0, 1, stride=1, stride_axis=0)
        zero = jnp.zeros((TILE, TILE), BF)
        for ref, whole in zip((wh, wl), parts(band_c)):
            b_prev = jnp.where(before, whole, zero)
            b_next = jnp.where(after, whole, zero)
            b_here = jnp.where(before | after, zero, whole)
            ref[slot, 0:TILE, 0:TILE] = b_here
            ref[slot, TILE:, TILE:] = b_here
            ref[slot, 0:TILE, TILE:] = b_prev
            ref[slot, TILE:, 0:TILE] = b_next

    def build_own(v, carry):
        build(0, v, v)
        return carry

    def build_far(v, carry):
        build(1, v, visits + v)
        return carry

    lax.fori_loop(0, visits, build_own, 0)
    load_img.wait()

    def smear(slot, matrix, start, depth, rows):
        both = mm(matrix[slot, :, 0:depth], x[slot, pl.ds(al(start), depth), :])
        return both[0:rows] + both[rows:]

    def put(slot, start, rows, value):
        for n, block in enumerate(cols_filter(value, wh[slot], wl[slot])):
            vals[slot, pl.ds(al(start), rows), n * TILE:(n + 1) * TILE] = block

    def convolve(i, carry):
        slots = [i * 2 + u for u in range(2)]
        smeared = [smear(s, trow, (1 - exp) * PAD, kmain, main) for s in slots]
        for s, value in zip(slots, smeared):
            put(s, (1 - exp) * PAD, main, value)
        return carry

    lax.fori_loop(0, visits // 2, convolve, 0)
    send_taps.wait_recv()
    lax.fori_loop(0, visits, build_far, 0)
    send_far.wait_recv()
    lax.fori_loop(visits // 2, visits, convolve, 0)
    build(0, visits, HALVES * visits)

    def convolve_edge(c, carry):
        @pl.when(has_halo)
        def _():
            for source in range(HALVES):
                halo_wait(source, c).wait_recv()
        slots = [k * visits + c * 2 + u for k in range(HALVES) for u in range(2)]
        smeared = [smear(s, tbnd, exp * main, kbnd, PAD) for s in slots]
        for s, value in zip(slots, smeared):
            put(s, exp * main, PAD, value)
        return carry

    def halo_wait(source, c):
        land_at = al(exp * (PAD + mine))
        piece = x.at[pl.ds(source * visits + c * 2, 2), pl.ds(land_at, PAD), :]
        return remote(piece, piece, halo_send.at[0, c], halo_recv.at[source, c], other_core)

    lax.fori_loop(0, chunks, convolve_edge, 0)
    load_mask.wait()
    send_fmask.wait_recv()

    def select(start):
        span = 2 * TILE

        def group(g, carry):
            rows = pl.ds(pl.multiple_of(start + (g // (columns // span)) * 8, 8), 8)
            cols = pl.ds(pl.multiple_of(lax.rem(g, columns // span) * span, span), span)
            upper, lower, total, count = None, None, None, None
            for first in range(0, HALVES * visits, REJECT):
                tops, bottoms = [], []
                for v in range(first, first + REJECT):
                    value, used = vals[v, rows, cols], msk[v, rows, cols]
                    live = used == 1
                    tops.append(jnp.where(live, value, -SENTINEL))
                    bottoms.append(jnp.where(live, value, SENTINEL))
                    kept = jnp.where(live, value, 0.0)
                    total = kept if total is None else total + kept
                    count = used if count is None else count + used
                tops, bottoms = sort4(*tops), sort4(*bottoms)
                if upper is None:
                    upper, lower = tops, bottoms
                else:
                    upper = [jnp.maximum(a, b) for a, b in zip(upper, tops[::-1])]
                    lower = [jnp.minimum(a, b) for a, b in zip(lower, bottoms[::-1])]
                    if first + REJECT < HALVES * visits:
                        upper, lower = resort4(*upper), resort4(*lower)
            upper_sum = (upper[0] + upper[1]) + (upper[2] + upper[3])
            lower_sum = (lower[0] + lower[1]) + (lower[2] + lower[3])
            spot = pl.ds(pl.multiple_of(PAD + exp * mine + start + (g // (columns // span)) * 8, 8), 8)
            cpad[spot, cols] = (total - upper_sum - lower_sum) / (count.astype(F32) - 2 * REJECT)
            return carry

        lax.fori_loop(0, (PAD // 8) * (columns // span), group, 0)

    def share(k):
        def at(core):
            return al(PAD + jnp.where(core == 0, mine - PAD - k * PAD, mine + k * PAD))
        rows = pl.ds(at(exp), PAD)
        return remote(cpad.at[rows, :], cpad.at[rows, :], share_send.at[k], share_recv.at[k], other_core)

    def select_block(k):
        select(jnp.where(exp == 0, mine - PAD - k * PAD, k * PAD))

    edge = main // PAD
    co_halo = remote(
        cpad.at[pl.ds(al(PAD + exp * (height - PAD)), PAD), :],
        cpad.at[pl.ds(al((1 - exp) * (PAD + height)), PAD), :],
        co_send, co_recv,
        {"sky": lax.rem(sky + jnp.where(exp == 0, n_sky - 1, 1), n_sky), "exp": 1 - exp},
    )
    select_block(edge)

    @pl.when(has_halo)
    def _():
        co_halo.start()
    share(edge).start()
    for k in range(edge):
        select_block(k)
        share(k).start()

    psf = HALVES * visits

    def filter_rows(first, depth, matrix, rows, put_at):
        high, low = parts(cpad[pl.ds(al(first), depth), :])
        both = mm(matrix[psf, :, 0:depth], high)
        smeared = both[0:rows] + both[rows:] + mm(matrix[psf, 0:rows, 0:depth], low)
        partial = jnp.zeros((8, TILE), F32)
        for n, block in enumerate(cols_filter(smeared, wh[psf], wl[psf])):
            squared = block * block
            energy[put_at:put_at + rows, n * TILE:(n + 1) * TILE] = squared
            for r in range(0, rows, 8):
                partial = partial + squared[r:r + 8]
        return partial

    steps = [(db, dx) for db in range(n_band) for dx in range(HALVES)][1:]

    def send_energy(slot, piece):
        db, dx = steps[slot]
        target = lax.rem(band + db, n_band)
        rows = (pl.ds(0, main), pl.ds(main, PAD))[piece]
        return remote(
            energy.at[rows, pl.ds(pl.multiple_of(target * width, TILE), width)],
            land.at[slot, rows, :],
            en_send.at[slot, piece], en_recv.at[slot, piece],
            {"band": target, "exp": exp if dx == 0 else 1 - exp},
        )

    share(0).wait_recv()
    partial = filter_rows(exp * mine + (1 - exp) * PAD, kmain, trow, main, 0)
    for slot in range(len(steps)):
        send_energy(slot, 0).start()
    for k in range(1, edge + 1):
        share(k).wait_recv()
    store_coadd = pltpu.make_async_copy(cpad.at[pl.ds(PAD, height), :], coadd_out.at[0], out_sem.at[0])
    store_coadd.start()

    @pl.when(has_halo)
    def _():
        co_halo.wait_recv()
    partial = partial + filter_rows(exp * (mine + main), kbnd, tbnd, PAD, main)
    sums[pl.ds(me, 1)] = partial[None]

    def send_sum(step):
        return remote(sums.at[me], sums.at[me], sum_send.at[step - 1], sum_recv.at[step - 1], peer_of(step))

    def start_sum(step, carry):
        send_sum(step).start()
        return carry

    lax.fori_loop(1, n_peer, start_sum, 0)
    for slot in range(len(steps)):
        send_energy(slot, 1).start()

    def wait_sum(step, carry):
        send_sum(step).wait_recv()
        return carry

    lax.fori_loop(1, n_peer, wait_sum, 0)
    pixels = height * n_sky * columns

    def inverse(source):
        total = None
        for s in range(n_sky):
            for e in range(HALVES):
                term = sums[(s * n_band + source) * HALVES + e]
                total = term if total is None else total + term
        return 1.0 / (jnp.sum(total, keepdims=True) / pixels + EPSILON)

    inv = [inverse(lax.rem(band + n_band - db, n_band)) for db in range(n_band)]
    for slot in range(len(steps)):
        for piece in range(2):
            send_energy(slot, piece).wait_recv()
    own = energy[:, pl.ds(pl.multiple_of(band * width, TILE), width)] * inv[0]
    far = land[0] * inv[0]
    for db in range(1, n_band):
        own = own + land[db * 2 - 1] * inv[db]
        far = far + land[db * 2] * inv[db]
    for core, value in ((exp, own), (1 - exp, far)):
        det[pl.ds(al(core * mine + (1 - core) * PAD), main), :] = value[0:main]
        det[pl.ds(al(core * (mine + main)), PAD), :] = value[main:]
    store_det = pltpu.make_async_copy(det, det_out, out_sem.at[1])
    store_det.start()

    def drain(c, carry):
        @pl.when(has_after)
        def _():
            halo(0, c).wait_send()

        @pl.when(has_before)
        def _():
            halo(1, c).wait_send()
        return carry

    lax.fori_loop(0, chunks, drain, 0)
    send_far.wait_send()
    send_fmask.wait_send()
    send_taps.wait_send()

    @pl.when(has_halo)
    def _():
        co_halo.wait_send()
    for k in range(edge + 1):
        share(k).wait_send()

    def drain_sum(step, carry):
        send_sum(step).wait_send()
        return carry

    lax.fori_loop(1, n_peer, drain_sum, 0)
    for slot in range(len(steps)):
        for piece in range(2):
            send_energy(slot, piece).wait_send()
    store_coadd.wait()
    store_det.wait()


def hand_on(coadd_in, det_in, coadd_out, det_out, sem):
    copies = [
        pltpu.make_async_copy(coadd_in, coadd_out, sem.at[0]),
        pltpu.make_async_copy(det_in, det_out, sem.at[1]),
    ]
    for copy in copies:
        copy.start()
    for copy in copies:
        copy.wait()


def solution(mesh):
    n_sky, n_band = mesh.shape["sky"], mesh.shape["band"]

    def on_device(images, valid_mask, row_kernel, col_kernel, exp_group, zero_point, psf_row, psf_col):
        _, visits, height, columns = images.shape
        assert height == TILE and mesh.shape["exp"] == HALVES and visits % 2 == 0
        assert visits + 1 <= 16
        width = columns // n_band
        mine = height // HALVES
        main = mine - PAD
        frame = mine + 2 * PAD
        chunks = visits // 2
        slots = HALVES * visits
        n_peer = n_sky * n_band * HALVES
        n_step = n_band * HALVES - 1
        blocks = mine // PAD
        hbm, anywhere = (pl.BlockSpec(memory_space=space) for space in (pltpu.HBM, pl.ANY))
        dma = pltpu.SemaphoreType.DMA
        shapes = (
            jax.ShapeDtypeStruct((1, height, columns), F32),
            jax.ShapeDtypeStruct((height, width), F32),
        )
        coadd, det = pl.pallas_call(
            functools.partial(kernel, n_sky, n_band),
            out_shape=tuple(pltpu.VMEM(s.shape, s.dtype) for s in shapes),
            in_specs=[hbm] * 8,
            out_specs=(anywhere, anywhere),
            scratch_shapes=[
                pltpu.VMEM((visits, 1, TAPS), F32),
                pltpu.VMEM((visits, 1, TAPS), F32),
                pltpu.VMEM((1, TAPS), F32),
                pltpu.VMEM((1, TAPS), F32),
                pltpu.SMEM(exp_group.shape, jnp.int32),
                pltpu.SMEM(zero_point.shape, F32),
                pltpu.VMEM((slots, frame, columns), BF),
                pltpu.VMEM((slots, mine, columns), jnp.int32),
                pltpu.VMEM((2, 2, 16, TILE), F32),
                pltpu.VMEM((slots + 1, 2 * main, TILE), BF),
                pltpu.VMEM((slots + 1, 2 * PAD, TILE), BF),
                pltpu.VMEM((slots + 1, 2 * TILE, 2 * TILE), BF),
                pltpu.VMEM((slots + 1, 2 * TILE, 2 * TILE), BF),
                pltpu.VMEM((slots, mine, columns), F32),
                pltpu.VMEM((height + 2 * PAD, columns), F32),
                pltpu.VMEM((mine, columns), F32),
                pltpu.VMEM((n_step, mine, width), F32),
                pltpu.VMEM((n_peer, 8, TILE), F32),
                pltpu.VMEM((height, width), F32),
                dma((6,)), dma, dma, dma, dma, dma, dma, dma, dma,
                dma((2, chunks)), dma((2, chunks)), dma((blocks,)), dma((blocks,)), dma, dma,
                dma((n_peer - 1,)), dma((n_peer - 1,)), dma((n_step, 2)), dma((n_step, 2)), dma((2,)),
            ],
            compiler_params=pltpu.CompilerParams(
                collective_id=0, has_side_effects=True, vmem_limit_bytes=48 << 20
            ),
        )(*(pltpu.with_memory_space_constraint(a, pltpu.HBM) for a in (images, valid_mask, jnp.swapaxes(row_kernel, 0, 1), jnp.swapaxes(col_kernel, 0, 1), psf_row, psf_col, exp_group, zero_point)))
        return pl.pallas_call(
            hand_on,
            out_shape=shapes,
            in_specs=[anywhere] * 2,
            out_specs=(anywhere, anywhere),
            scratch_shapes=[dma((2,))],
            compiler_params=pltpu.CompilerParams(vmem_limit_bytes=1 << 20),
        )(coadd, det)

    placed = (
        P("band", "exp", ("patch", "sky"), None),
        P("band", "exp", ("patch", "sky"), None),
        P("band", "exp", None),
        P("band", "exp", None),
        P("band", "exp"),
        P("band", None),
        P("band", None),
        P("band", None),
    )
    return jax.shard_map(
        on_device,
        mesh=mesh,
        in_specs=placed,
        out_specs=(P("band", ("patch", "sky"), None), P(("patch", "sky"), "band")),
        check_vma=False,
    )
```

```python
import functools

import jax
import jax.numpy as jnp
from jax import lax
from jax.experimental import pallas as pl
from jax.experimental.pallas import tpu as pltpu
from jax.sharding import PartitionSpec as P

MESH = pl.DeviceIdType.MESH
HALF = 15
REJECT = 4
TAPS = 31
SENTINEL = 1e30
EPSILON = 1e-05
PAD = 16
TILE = 128
HALVES = 2
STACK = 5
AHEAD = 2
BF = jnp.bfloat16
F32 = jnp.float32


def parts(value):
    high = value.astype(BF)
    return high, (value - high.astype(F32)).astype(BF)


def mm(a, b):
    return jnp.dot(a, b, preferred_element_type=F32)


def cols_filter(value, matrix):
    rows, columns = value.shape
    blocks = columns // TILE
    high, low = parts(value)
    zero = jnp.zeros((rows, TILE), BF)
    cut = [slice(n * TILE, (n + 1) * TILE) for n in range(blocks)]
    left = [jnp.concatenate([high[:, at], high[:, at]], axis=1) for at in cut]
    left += [jnp.concatenate([low[:, at], zero], axis=1) for at in cut]
    spread = mm(jnp.concatenate(left, axis=0), matrix)
    spread = [spread[n * rows:(n + 1) * rows] + spread[(blocks + n) * rows:(blocks + n + 1) * rows] for n in range(blocks)]
    joined = [spread[0][:, 0:TILE]]
    for n in range(1, blocks):
        joined.append(spread[n][:, 0:TILE] + spread[n - 1][:, TILE:])
    joined.append(spread[-1][:, TILE:])
    joined = [pltpu.roll(part, TILE // 2, 1) for part in joined]
    first = lax.broadcasted_iota(jnp.int32, (rows, TILE), 1) < TILE // 2
    return [jnp.where(first, joined[n], joined[n + 1]) for n in range(blocks)]


def swap(a, b):
    return jnp.minimum(a, b), jnp.maximum(a, b)


def sort4(a, b, c, d):
    a, b = swap(a, b)
    c, d = swap(c, d)
    a, c = swap(a, c)
    b, d = swap(b, d)
    b, c = swap(b, c)
    return [a, b, c, d]


def resort4(a, b, c, d):
    a, c = swap(a, c)
    b, d = swap(b, d)
    a, b = swap(a, b)
    c, d = swap(c, d)
    return [a, b, c, d]


def kernel(
    n_sky, n_band,
    img, mask, rk_in, ck_in, pr_in, pc_in, eg_in, zp_in,
    coadd_out, det_out,
    rk, ck, pr, pc, eg, zp, x, msk, taps, trow, tedge, tpsf, wide, vals, cpad, energy, land, sums, det,
    arg_sem, img_sem, mask_sem, tap_send, tap_recv, far_send, far_recv, fmask_send, fmask_recv,
    halo_send, halo_recv, share_send, share_recv, co_send, co_recv, sum_send, sum_recv, en_send, en_recv, out_sem,
):
    visits, height, columns = img.shape[1:]
    mine = height // HALVES
    main = mine - PAD
    frame = mine + 2 * PAD
    kmain, kbnd = main + 2 * PAD, 3 * PAD
    width = columns // n_band
    chunks = visits // STACK
    sky, band, exp = lax.axis_index("sky"), lax.axis_index("band"), lax.axis_index("exp")
    has_before, has_after = sky > 0, sky < n_sky - 1
    has_halo = jnp.where(exp == 0, sky, n_sky - 1 - sky) > 0
    n_peer = n_sky * n_band * HALVES
    me = (sky * n_band + band) * HALVES + exp

    def peer_of(step):
        peer = lax.rem(me + step, n_peer)
        chip = peer // HALVES
        return {"sky": chip // n_band, "band": lax.rem(chip, n_band), "exp": lax.rem(peer, HALVES)}

    other_core = {"exp": 1 - exp}

    def remote(source, target, send, recv, device):
        return pltpu.make_async_remote_copy(
            src_ref=source, dst_ref=target, send_sem=send, recv_sem=recv, device_id=device, device_id_type=MESH,
        )

    def al(value):
        return pl.multiple_of(value, PAD)

    small = [
        pltpu.make_async_copy(source, target, arg_sem.at[k])
        for k, (source, target) in enumerate(
            ((eg_in, eg), (zp_in, zp), (ck_in, ck), (pc_in, pc), (rk_in, rk), (pr_in, pr))
        )
    ]
    for copy in small:
        copy.start()

    barrier = pltpu.get_barrier_semaphore()

    def greet(step, carry):
        pl.semaphore_signal(barrier, inc=1, device_id=peer_of(step), device_id_type=MESH)
        return carry

    lax.fori_loop(1, n_peer, greet, 0)

    load_img = pltpu.make_async_copy(
        img.at[0, :, pl.ds(al(exp * (mine - PAD)), kmain), :],
        x.at[pl.ds(0, visits), pl.ds(al((1 - exp) * PAD), kmain), :], img_sem,
    )
    load_img.start()
    load_mask = pltpu.make_async_copy(
        mask.at[0, :, pl.ds(al(exp * mine), mine), :], msk.at[pl.ds(0, visits)], mask_sem
    )
    load_mask.start()
    pl.semaphore_wait(barrier, n_peer - 1)

    def halo(side, c):
        start, land_at = ((height - PAD, 0), (0, PAD + mine))[side]
        slot = jnp.where(exp == side, 0, visits) + c * STACK
        return remote(
            img.at[0, pl.ds(c * STACK, STACK), pl.ds(start, PAD), :],
            x.at[pl.ds(slot, STACK), pl.ds(land_at, PAD), :],
            halo_send.at[side, c], halo_recv.at[jnp.where(exp == side, 0, 1), c],
            {"sky": lax.rem(sky + (1, n_sky - 1)[side], n_sky), "exp": side},
        )

    def start_halo(c, carry):
        @pl.when(has_after)
        def _():
            halo(0, c).start()

        @pl.when(has_before)
        def _():
            halo(1, c).start()
        return carry

    lax.fori_loop(0, chunks, start_halo, 0)

    send_far = remote(
        img.at[0, :, pl.ds(al((1 - exp) * (mine - PAD)), kmain), :],
        x.at[pl.ds(visits, visits), pl.ds(al(exp * PAD), kmain), :],
        far_send, far_recv, other_core,
    )
    send_far.start()
    send_fmask = remote(
        mask.at[0, :, pl.ds(al((1 - exp) * mine), mine), :], msk.at[pl.ds(visits, visits)],
        fmask_send, fmask_recv, other_core,
    )
    send_fmask.start()

    taps[0] = jnp.zeros(taps.shape[1:], F32)
    for copy in small:
        copy.wait()
    for v in range(visits):
        taps[0, 0, v:v + 1, 0:TAPS] = rk[v]
    taps[0, 0, visits:visits + 1, 0:TAPS] = pr[...]
    for v in range(visits):
        taps[0, 1, v:v + 1, 0:TAPS] = ck[v] * zp[0, eg[0, v]]
    taps[0, 1, visits:visits + 1, 0:TAPS] = pc[...]
    at_row = lax.broadcasted_iota(jnp.int32, (TILE, TILE), 0)
    at_col = lax.broadcasted_iota(jnp.int32, (TILE, TILE), 1)
    flip = (at_col == TILE // 2 + HALF - at_row).astype(F32)
    taps[0, 1, :, 0:TILE] = jnp.dot(taps[0, 1, :, 0:TILE], flip, preferred_element_type=F32, precision=lax.Precision.HIGHEST)
    send_taps = remote(taps.at[0], taps.at[1], tap_send, tap_recv, other_core)
    send_taps.start()

    @pl.when(jnp.logical_not(has_halo))
    def _():
        x[:, pl.ds(al(exp * (PAD + mine)), PAD), :] = jnp.zeros((HALVES * visits, PAD, columns), BF)
        cpad[pl.ds(al(exp * (PAD + height)), PAD), :] = jnp.zeros((PAD, columns), F32)

    upward = (at_col > at_row).astype(F32).astype(BF)

    def slanted(origin, v, rows, lanes, shift):
        line = jnp.broadcast_to(taps[origin, 0, v:v + 1, 0:lanes], (rows, lanes))
        return pltpu.roll(line, shift, 1, stride=1, stride_axis=0)

    def build_wide(origin, v, slot):
        line = jnp.broadcast_to(taps[origin, 1, v:v + 1, 0:TILE], (TILE, TILE))
        line = pltpu.roll(line, 0, 1, stride=1, stride_axis=0)
        for n, part in enumerate(parts(line)):
            here = part * upward
            wide[slot, n * TILE:(n + 1) * TILE, 0:TILE] = here
            wide[slot, n * TILE:(n + 1) * TILE, TILE:] = part - here

    def build(origin, v):
        slot = origin * visits + v
        for n, part in enumerate(parts(slanted(origin, v, main, TILE, 1))):
            trow[slot, n * main:(n + 1) * main, :] = part
        group, j = divmod(slot, STACK)
        for n, part in enumerate(parts(slanted(origin, v, PAD, 2 * TILE, j * kbnd + 1))):
            tedge[group, (n * STACK + j) * PAD:(n * STACK + j + 1) * PAD, :] = part
        build_wide(origin, v, slot)

    def smear(slot):
        both = mm(trow[slot, :, 0:kmain], x[slot, pl.ds(al((1 - exp) * PAD), kmain), :])
        return both[0:main] + both[main:]

    def put(slot, start, rows, value):
        for n, block in enumerate(cols_filter(value, wide[slot])):
            vals[slot, pl.ds(al(start), rows), n * TILE:(n + 1) * TILE] = block

    def convolve(origin):
        waiting = []
        for v in range(visits):
            build(origin, v)
            slot = origin * visits + v
            waiting.append((slot, smear(slot)))
            if len(waiting) > AHEAD:
                done, value = waiting.pop(0)
                put(done, (1 - exp) * PAD, main, value)
        for done, value in waiting:
            put(done, (1 - exp) * PAD, main, value)

    load_img.wait()
    convolve(0)
    send_taps.wait_recv()
    send_far.wait_recv()
    convolve(1)

    psf = HALVES * visits
    build_wide(0, visits, psf)
    for rows, depth, at in ((main, kmain, 0), (PAD, kbnd, main)):
        pieces = [parts(slanted(0, visits, rows, 2 * TILE, j * depth + 1))[int(j == 2)] for j in range(3)]
        tpsf[at:at + rows, :] = pieces[0] + pieces[1] + pieces[2]

    def halo_wait(source, c):
        land_at = al(exp * (PAD + mine))
        piece = x.at[pl.ds(source * visits + c * STACK, STACK), pl.ds(land_at, PAD), :]
        return remote(piece, piece, halo_send.at[0, c], halo_recv.at[source, c], other_core)

    def smear_edge(group):
        first = group * STACK
        stacked = x[first:first + STACK, pl.ds(al(exp * main), kbnd), :].reshape(STACK * kbnd, columns)
        both = mm(tedge[group, :, 0:STACK * kbnd], stacked)
        return both[0:STACK * PAD] + both[STACK * PAD:]

    def put_edge(group, value):
        for u in range(STACK):
            put(group * STACK + u, exp * main, PAD, value[u * PAD:(u + 1) * PAD])

    held = None
    for c in range(chunks):
        for source in range(HALVES):
            @pl.when(has_halo)
            def _():
                halo_wait(source, c).wait_recv()
            group = source * chunks + c
            value = smear_edge(group)
            if held is not None:
                put_edge(*held)
            held = group, value
    put_edge(*held)
    load_mask.wait()
    send_fmask.wait_recv()

    def select(start):
        span = 2 * TILE

        def group(g, carry):
            rows = pl.ds(pl.multiple_of(start + (g // (columns // span)) * 8, 8), 8)
            cols = pl.ds(pl.multiple_of(lax.rem(g, columns // span) * span, span), span)
            upper, lower, total, count = None, None, None, None
            for first in range(0, HALVES * visits, REJECT):
                tops, bottoms = [], []
                for v in range(first, first + REJECT):
                    value, used = vals[v, rows, cols], msk[v, rows, cols]
                    live = used == 1
                    tops.append(jnp.where(live, value, -SENTINEL))
                    bottoms.append(jnp.where(live, value, SENTINEL))
                    kept = jnp.where(live, value, 0.0)
                    total = kept if total is None else total + kept
                    count = used if count is None else count + used
                tops, bottoms = sort4(*tops), sort4(*bottoms)
                if upper is None:
                    upper, lower = tops, bottoms
                else:
                    upper = [jnp.maximum(a, b) for a, b in zip(upper, tops[::-1])]
                    lower = [jnp.minimum(a, b) for a, b in zip(lower, bottoms[::-1])]
                    if first + REJECT < HALVES * visits:
                        upper, lower = resort4(*upper), resort4(*lower)
            upper_sum = (upper[0] + upper[1]) + (upper[2] + upper[3])
            lower_sum = (lower[0] + lower[1]) + (lower[2] + lower[3])
            spot = pl.ds(pl.multiple_of(PAD + exp * mine + start + (g // (columns // span)) * 8, 8), 8)
            cpad[spot, cols] = (total - upper_sum - lower_sum) / (count.astype(F32) - 2 * REJECT)
            return carry

        lax.fori_loop(0, (PAD // 8) * (columns // span), group, 0, unroll=2)

    def share(k):
        def at(core):
            return al(PAD + jnp.where(core == 0, mine - PAD - k * PAD, mine + k * PAD))
        rows = pl.ds(at(exp), PAD)
        return remote(cpad.at[rows, :], cpad.at[rows, :], share_send.at[k], share_recv.at[k], other_core)

    def select_block(k):
        select(jnp.where(exp == 0, mine - PAD - k * PAD, k * PAD))

    edge = main // PAD
    co_halo = remote(
        cpad.at[pl.ds(al(PAD + exp * (height - PAD)), PAD), :],
        cpad.at[pl.ds(al((1 - exp) * (PAD + height)), PAD), :],
        co_send, co_recv,
        {"sky": lax.rem(sky + jnp.where(exp == 0, n_sky - 1, 1), n_sky), "exp": 1 - exp},
    )
    select_block(edge)

    @pl.when(has_halo)
    def _():
        co_halo.start()
    share(edge).start()
    for k in range(edge):
        select_block(k)
        share(k).start()

    def filter_rows(first, depth, rows, put_at):
        high, low = parts(cpad[pl.ds(al(first), depth), :])
        smeared = mm(tpsf[put_at:put_at + rows, 0:3 * depth], jnp.concatenate([high, low, high], axis=0))
        partial = jnp.zeros((8, TILE), F32)
        for n, block in enumerate(cols_filter(smeared, wide[psf])):
            squared = block * block
            energy[put_at:put_at + rows, n * TILE:(n + 1) * TILE] = squared
            for r in range(0, rows, 8):
                partial = partial + squared[r:r + 8]
        return partial

    steps = [(db, dx) for db in range(n_band) for dx in range(HALVES)][1:]

    def send_energy(slot, piece):
        db, dx = steps[slot]
        target = lax.rem(band + db, n_band)
        rows = (pl.ds(0, main), pl.ds(main, PAD))[piece]
        return remote(
            energy.at[rows, pl.ds(pl.multiple_of(target * width, TILE), width)],
            land.at[slot, rows, :],
            en_send.at[slot, piece], en_recv.at[slot, piece],
            {"band": target, "exp": exp if dx == 0 else 1 - exp},
        )

    share(0).wait_recv()
    partial = filter_rows(exp * mine + (1 - exp) * PAD, kmain, main, 0)
    for slot in range(len(steps)):
        send_energy(slot, 0).start()
    for k in range(1, edge + 1):
        share(k).wait_recv()
    store_coadd = pltpu.make_async_copy(cpad.at[pl.ds(PAD, height), :], coadd_out.at[0], out_sem.at[0])
    store_coadd.start()

    @pl.when(has_halo)
    def _():
        co_halo.wait_recv()
    partial = partial + filter_rows(exp * (mine + main), kbnd, PAD, main)
    sums[pl.ds(me, 1)] = partial[None]

    def send_sum(step):
        return remote(sums.at[me], sums.at[me], sum_send.at[step - 1], sum_recv.at[step - 1], peer_of(step))

    def start_sum(step, carry):
        send_sum(step).start()
        return carry

    lax.fori_loop(1, n_peer, start_sum, 0)
    for slot in range(len(steps)):
        send_energy(slot, 1).start()

    def wait_sum(step, carry):
        send_sum(step).wait_recv()
        return carry

    lax.fori_loop(1, n_peer, wait_sum, 0)
    pixels = height * n_sky * columns

    def inverse(source):
        total = None
        for s in range(n_sky):
            for e in range(HALVES):
                term = sums[(s * n_band + source) * HALVES + e]
                total = term if total is None else total + term
        return 1.0 / (jnp.sum(total, keepdims=True) / pixels + EPSILON)

    inv = [inverse(lax.rem(band + n_band - db, n_band)) for db in range(n_band)]
    for slot in range(len(steps)):
        for piece in range(2):
            send_energy(slot, piece).wait_recv()
    own = energy[:, pl.ds(pl.multiple_of(band * width, TILE), width)] * inv[0]
    far = land[0] * inv[0]
    for db in range(1, n_band):
        own = own + land[db * 2 - 1] * inv[db]
        far = far + land[db * 2] * inv[db]
    for core, value in ((exp, own), (1 - exp, far)):
        det[pl.ds(al(core * mine + (1 - core) * PAD), main), :] = value[0:main]
        det[pl.ds(al(core * (mine + main)), PAD), :] = value[main:]
    store_det = pltpu.make_async_copy(det, det_out, out_sem.at[1])
    store_det.start()

    def drain(c, carry):
        @pl.when(has_after)
        def _():
            halo(0, c).wait_send()

        @pl.when(has_before)
        def _():
            halo(1, c).wait_send()
        return carry

    lax.fori_loop(0, chunks, drain, 0)
    send_far.wait_send()
    send_fmask.wait_send()
    send_taps.wait_send()

    @pl.when(has_halo)
    def _():
        co_halo.wait_send()
    for k in range(edge + 1):
        share(k).wait_send()

    def drain_sum(step, carry):
        send_sum(step).wait_send()
        return carry

    lax.fori_loop(1, n_peer, drain_sum, 0)
    for slot in range(len(steps)):
        for piece in range(2):
            send_energy(slot, piece).wait_send()
    store_coadd.wait()
    store_det.wait()


def hand_on(coadd_in, det_in, coadd_out, det_out, sem):
    copies = [
        pltpu.make_async_copy(coadd_in, coadd_out, sem.at[0]),
        pltpu.make_async_copy(det_in, det_out, sem.at[1]),
    ]
    for copy in copies:
        copy.start()
    for copy in copies:
        copy.wait()


def solution(mesh):
    n_sky, n_band = mesh.shape["sky"], mesh.shape["band"]

    def on_device(images, valid_mask, row_kernel, col_kernel, exp_group, zero_point, psf_row, psf_col):
        _, visits, height, columns = images.shape
        assert height == TILE and mesh.shape["exp"] == HALVES and visits % STACK == 0
        assert visits + 1 <= 16
        width = columns // n_band
        mine = height // HALVES
        main = mine - PAD
        frame = mine + 2 * PAD
        chunks = visits // STACK
        slots = HALVES * visits
        n_peer = n_sky * n_band * HALVES
        n_step = n_band * HALVES - 1
        blocks = mine // PAD
        hbm, anywhere = (pl.BlockSpec(memory_space=space) for space in (pltpu.HBM, pl.ANY))
        dma = pltpu.SemaphoreType.DMA
        shapes = (
            jax.ShapeDtypeStruct((1, height, columns), F32),
            jax.ShapeDtypeStruct((height, width), F32),
        )
        coadd, det = pl.pallas_call(
            functools.partial(kernel, n_sky, n_band),
            out_shape=tuple(pltpu.VMEM(s.shape, s.dtype) for s in shapes),
            in_specs=[hbm] * 8,
            out_specs=(anywhere, anywhere),
            scratch_shapes=[
                pltpu.VMEM((visits, 1, TAPS), F32),
                pltpu.VMEM((visits, 1, TAPS), F32),
                pltpu.VMEM((1, TAPS), F32),
                pltpu.VMEM((1, TAPS), F32),
                pltpu.SMEM(exp_group.shape, jnp.int32),
                pltpu.SMEM(zero_point.shape, F32),
                pltpu.VMEM((slots, frame, columns), BF),
                pltpu.VMEM((slots, mine, columns), jnp.int32),
                pltpu.VMEM((2, 2, 16, 2 * TILE), F32),
                pltpu.VMEM((slots, 2 * main, TILE), BF),
                pltpu.VMEM((slots // STACK, 2 * STACK * PAD, 2 * TILE), BF),
                pltpu.VMEM((mine, 2 * TILE), BF),
                pltpu.VMEM((slots + 1, 2 * TILE, 2 * TILE), BF),
                pltpu.VMEM((slots, mine, columns), F32),
                pltpu.VMEM((height + 2 * PAD, columns), F32),
                pltpu.VMEM((mine, columns), F32),
                pltpu.VMEM((n_step, mine, width), F32),
                pltpu.VMEM((n_peer, 8, TILE), F32),
                pltpu.VMEM((height, width), F32),
                dma((6,)), dma, dma, dma, dma, dma, dma, dma, dma,
                dma((2, chunks)), dma((2, chunks)), dma((blocks,)), dma((blocks,)), dma, dma,
                dma((n_peer - 1,)), dma((n_peer - 1,)), dma((n_step, 2)), dma((n_step, 2)), dma((2,)),
            ],
            compiler_params=pltpu.CompilerParams(
                collective_id=0, has_side_effects=True, vmem_limit_bytes=48 << 20
            ),
        )(*(
            pltpu.with_memory_space_constraint(array, pltpu.HBM)
            for array in (
                images, valid_mask, jnp.swapaxes(row_kernel, 0, 1), jnp.swapaxes(col_kernel, 0, 1),
                psf_row, psf_col, exp_group, zero_point,
            )
        ))
        return pl.pallas_call(
            hand_on,
            out_shape=shapes,
            in_specs=[anywhere] * 2,
            out_specs=(anywhere, anywhere),
            scratch_shapes=[dma((2,))],
            compiler_params=pltpu.CompilerParams(vmem_limit_bytes=1 << 20),
        )(coadd, det)

    placed = (
        P("band", "exp", ("patch", "sky"), None),
        P("band", "exp", ("patch", "sky"), None),
        P("band", "exp", None),
        P("band", "exp", None),
        P("band", "exp"),
        P("band", None),
        P("band", None),
        P("band", None),
    )
    return jax.shard_map(
        on_device,
        mesh=mesh,
        in_specs=placed,
        out_specs=(P("band", ("patch", "sky"), None), P(("patch", "sky"), "band")),
        check_vma=False,
    )
```

```python
import functools

import jax
import jax.numpy as jnp
from jax import lax
from jax.experimental import pallas as pl
from jax.experimental.pallas import tpu as pltpu
from jax.sharding import PartitionSpec as P

MESH = pl.DeviceIdType.MESH
HALF = 15
REJECT = 4
TAPS = 31
SENTINEL = 1e30
EPSILON = 1e-05
PAD = 16
TILE = 128
HALVES = 2
STACK = 5
AHEAD = 2
BF = jnp.bfloat16
F32 = jnp.float32


def parts(value):
    high = value.astype(BF)
    return high, (value - high.astype(F32)).astype(BF)


def mm(a, b):
    return jnp.dot(a, b, preferred_element_type=F32)


def cols_filter(value, matrix):
    rows, columns = value.shape
    blocks = columns // TILE
    high, low = parts(value)
    zero = jnp.zeros((rows, TILE), BF)
    cut = [slice(n * TILE, (n + 1) * TILE) for n in range(blocks)]
    left = [jnp.concatenate([high[:, at], high[:, at]], axis=1) for at in cut]
    left += [jnp.concatenate([low[:, at], zero], axis=1) for at in cut]
    spread = mm(jnp.concatenate(left, axis=0), matrix)
    spread = [spread[n * rows:(n + 1) * rows] + spread[(blocks + n) * rows:(blocks + n + 1) * rows] for n in range(blocks)]
    joined = [spread[0][:, 0:TILE]]
    for n in range(1, blocks):
        joined.append(spread[n][:, 0:TILE] + spread[n - 1][:, TILE:])
    joined.append(spread[-1][:, TILE:])
    joined = [pltpu.roll(part, TILE // 2, 1) for part in joined]
    first = lax.broadcasted_iota(jnp.int32, (rows, TILE), 1) < TILE // 2
    return [jnp.where(first, joined[n], joined[n + 1]) for n in range(blocks)]


def swap(a, b):
    return jnp.minimum(a, b), jnp.maximum(a, b)


def sort4(a, b, c, d):
    a, b = swap(a, b)
    c, d = swap(c, d)
    a, c = swap(a, c)
    b, d = swap(b, d)
    b, c = swap(b, c)
    return [a, b, c, d]


def resort4(a, b, c, d):
    a, c = swap(a, c)
    b, d = swap(b, d)
    a, b = swap(a, b)
    c, d = swap(c, d)
    return [a, b, c, d]


def kernel(
    n_sky, n_band,
    img, mask, rk_in, ck_in, pr_in, pc_in, eg_in, zp_in,
    coadd_out, det_out,
    rk, ck, pr, pc, eg, zp, x, msk, taps, trow, tedge, tpsf, wide, vals, cpad, energy, land, sums, det,
    arg_sem, img_sem, mask_sem, tap_send, tap_recv, far_send, far_recv, fmask_send, fmask_recv,
    halo_send, halo_recv, share_send, share_recv, co_send, co_recv, sum_send, sum_recv, en_send, en_recv, out_sem, token,
):
    visits, height, columns = img.shape[1:]
    mine = height // HALVES
    main = mine - PAD
    frame = mine + 2 * PAD
    kmain, kbnd = main + 2 * PAD, 3 * PAD
    width = columns // n_band
    chunks = visits // STACK
    sky, band, exp = lax.axis_index("sky"), lax.axis_index("band"), lax.axis_index("exp")
    has_before, has_after = sky > 0, sky < n_sky - 1
    has_halo = jnp.where(exp == 0, sky, n_sky - 1 - sky) > 0
    n_peer = n_sky * n_band * HALVES
    me = (sky * n_band + band) * HALVES + exp

    def peer_of(step):
        peer = lax.rem(me + step, n_peer)
        chip = peer // HALVES
        return {"sky": chip // n_band, "band": lax.rem(chip, n_band), "exp": lax.rem(peer, HALVES)}

    other_core = {"exp": 1 - exp}

    def remote(source, target, send, recv, device):
        return pltpu.make_async_remote_copy(
            src_ref=source, dst_ref=target, send_sem=send, recv_sem=recv, device_id=device, device_id_type=MESH,
        )

    def al(value):
        return pl.multiple_of(value, PAD)

    small = [
        pltpu.make_async_copy(source, target, arg_sem.at[k])
        for k, (source, target) in enumerate(
            ((eg_in, eg), (zp_in, zp), (ck_in, ck), (pc_in, pc), (rk_in, rk), (pr_in, pr))
        )
    ]
    for copy in small:
        copy.start()

    barrier = pltpu.get_barrier_semaphore()

    def beside(side):
        return lax.rem(sky + (1, n_sky - 1)[side], n_sky)

    exists = (has_after, has_before)
    for side in range(2):
        @pl.when(exists[side])
        def _():
            for core in range(HALVES):
                pl.semaphore_signal(barrier, inc=1, device_id={"sky": beside(side), "exp": core}, device_id_type=MESH)
    pl.semaphore_signal(barrier, inc=1, device_id=other_core, device_id_type=MESH)
    for db in range(1, n_band):
        for core in range(HALVES):
            pl.semaphore_signal(
                barrier, inc=1, device_id={"band": lax.rem(band + db, n_band), "exp": core}, device_id_type=MESH
            )

    load_img = pltpu.make_async_copy(
        img.at[0, :, pl.ds(al(exp * (mine - PAD)), kmain), :],
        x.at[pl.ds(0, visits), pl.ds(al((1 - exp) * PAD), kmain), :], img_sem,
    )
    load_img.start()
    load_mask = pltpu.make_async_copy(
        mask.at[0, :, pl.ds(al(exp * mine), mine), :], msk.at[pl.ds(0, visits)], mask_sem
    )
    load_mask.start()
    greeted = sum(jnp.where(there, HALVES, 0) for there in exists)
    pl.semaphore_wait(barrier, greeted + 1 + HALVES * (n_band - 1))

    rounds = n_sky - 1

    def tell():
        for side in range(2):
            @pl.when(exists[side])
            def _():
                pl.semaphore_signal(token.at[side], inc=1, device_id={"sky": beside(side)}, device_id_type=MESH)

    def hear():
        for side in range(2):
            @pl.when(exists[1 - side])
            def _():
                pl.semaphore_wait(token.at[side], 1)

    def halo(side, c):
        start, land_at = ((height - PAD, 0), (0, PAD + mine))[side]
        slot = jnp.where(exp == side, 0, visits) + c * STACK
        return remote(
            img.at[0, pl.ds(c * STACK, STACK), pl.ds(start, PAD), :],
            x.at[pl.ds(slot, STACK), pl.ds(land_at, PAD), :],
            halo_send.at[side, c], halo_recv.at[jnp.where(exp == side, 0, 1), c],
            {"sky": beside(side), "exp": side},
        )

    def start_halo(c, carry):
        @pl.when(has_after)
        def _():
            halo(0, c).start()

        @pl.when(has_before)
        def _():
            halo(1, c).start()
        return carry

    lax.fori_loop(0, chunks, start_halo, 0)

    send_far = remote(
        img.at[0, :, pl.ds(al((1 - exp) * (mine - PAD)), kmain), :],
        x.at[pl.ds(visits, visits), pl.ds(al(exp * PAD), kmain), :],
        far_send, far_recv, other_core,
    )
    send_far.start()
    send_fmask = remote(
        mask.at[0, :, pl.ds(al((1 - exp) * mine), mine), :], msk.at[pl.ds(visits, visits)],
        fmask_send, fmask_recv, other_core,
    )
    send_fmask.start()
    tell()

    taps[0] = jnp.zeros(taps.shape[1:], F32)
    for copy in small:
        copy.wait()
    for v in range(visits):
        taps[0, 0, v:v + 1, 0:TAPS] = rk[v]
    taps[0, 0, visits:visits + 1, 0:TAPS] = pr[...]
    for v in range(visits):
        taps[0, 1, v:v + 1, 0:TAPS] = ck[v] * zp[0, eg[0, v]]
    taps[0, 1, visits:visits + 1, 0:TAPS] = pc[...]
    at_row = lax.broadcasted_iota(jnp.int32, (TILE, TILE), 0)
    at_col = lax.broadcasted_iota(jnp.int32, (TILE, TILE), 1)
    flip = (at_col == TILE // 2 + HALF - at_row).astype(F32)
    taps[0, 1, :, 0:TILE] = jnp.dot(taps[0, 1, :, 0:TILE], flip, preferred_element_type=F32, precision=lax.Precision.HIGHEST)
    send_taps = remote(taps.at[0], taps.at[1], tap_send, tap_recv, other_core)
    send_taps.start()

    @pl.when(jnp.logical_not(has_halo))
    def _():
        x[:, pl.ds(al(exp * (PAD + mine)), PAD), :] = jnp.zeros((HALVES * visits, PAD, columns), BF)
        cpad[pl.ds(al(exp * (PAD + height)), PAD), :] = jnp.zeros((PAD, columns), F32)

    upward = (at_col > at_row).astype(F32).astype(BF)

    def slanted(origin, v, rows, lanes, shift):
        line = jnp.broadcast_to(taps[origin, 0, v:v + 1, 0:lanes], (rows, lanes))
        return pltpu.roll(line, shift, 1, stride=1, stride_axis=0)

    def build_wide(origin, v, slot):
        line = jnp.broadcast_to(taps[origin, 1, v:v + 1, 0:TILE], (TILE, TILE))
        line = pltpu.roll(line, 0, 1, stride=1, stride_axis=0)
        for n, part in enumerate(parts(line)):
            here = part * upward
            wide[slot, n * TILE:(n + 1) * TILE, 0:TILE] = here
            wide[slot, n * TILE:(n + 1) * TILE, TILE:] = part - here

    def build(origin, v):
        slot = origin * visits + v
        for n, part in enumerate(parts(slanted(origin, v, main, TILE, 1))):
            trow[slot, n * main:(n + 1) * main, :] = part
        group, j = divmod(slot, STACK)
        for n, part in enumerate(parts(slanted(origin, v, PAD, 2 * TILE, j * kbnd + 1))):
            tedge[group, (n * STACK + j) * PAD:(n * STACK + j + 1) * PAD, :] = part
        build_wide(origin, v, slot)

    def smear(slot):
        both = mm(trow[slot, :, 0:kmain], x[slot, pl.ds(al((1 - exp) * PAD), kmain), :])
        return both[0:main] + both[main:]

    def put(slot, start, rows, value):
        for n, block in enumerate(cols_filter(value, wide[slot])):
            vals[slot, pl.ds(al(start), rows), n * TILE:(n + 1) * TILE] = block

    def convolve(origin):
        waiting = []
        for v in range(visits):
            build(origin, v)
            slot = origin * visits + v
            waiting.append((slot, smear(slot)))
            if len(waiting) > AHEAD:
                done, value = waiting.pop(0)
                put(done, (1 - exp) * PAD, main, value)
        for done, value in waiting:
            put(done, (1 - exp) * PAD, main, value)

    load_img.wait()
    convolve(0)
    if rounds > 1:
        hear()
        tell()
    send_taps.wait_recv()
    send_far.wait_recv()
    convolve(1)
    if rounds > 2:
        hear()
        tell()

    psf = HALVES * visits
    build_wide(0, visits, psf)
    for rows, depth, at in ((main, kmain, 0), (PAD, kbnd, main)):
        pieces = [parts(slanted(0, visits, rows, 2 * TILE, j * depth + 1))[int(j == 2)] for j in range(3)]
        tpsf[at:at + rows, :] = pieces[0] + pieces[1] + pieces[2]

    def halo_wait(source, c):
        land_at = al(exp * (PAD + mine))
        piece = x.at[pl.ds(source * visits + c * STACK, STACK), pl.ds(land_at, PAD), :]
        return remote(piece, piece, halo_send.at[0, c], halo_recv.at[source, c], other_core)

    def smear_edge(group):
        first = group * STACK
        stacked = x[first:first + STACK, pl.ds(al(exp * main), kbnd), :].reshape(STACK * kbnd, columns)
        both = mm(tedge[group, :, 0:STACK * kbnd], stacked)
        return both[0:STACK * PAD] + both[STACK * PAD:]

    def put_edge(group, value):
        for u in range(STACK):
            put(group * STACK + u, exp * main, PAD, value[u * PAD:(u + 1) * PAD])

    held = None
    for c in range(chunks):
        for source in range(HALVES):
            @pl.when(has_halo)
            def _():
                halo_wait(source, c).wait_recv()
            group = source * chunks + c
            value = smear_edge(group)
            if held is not None:
                put_edge(*held)
            held = group, value
    put_edge(*held)
    load_mask.wait()
    send_fmask.wait_recv()

    def select(start):
        span = 2 * TILE

        def group(g, carry):
            rows = pl.ds(pl.multiple_of(start + (g // (columns // span)) * 8, 8), 8)
            cols = pl.ds(pl.multiple_of(lax.rem(g, columns // span) * span, span), span)
            upper, lower, total, count = None, None, None, None
            for first in range(0, HALVES * visits, REJECT):
                tops, bottoms = [], []
                for v in range(first, first + REJECT):
                    value, used = vals[v, rows, cols], msk[v, rows, cols]
                    live = used == 1
                    tops.append(jnp.where(live, value, -SENTINEL))
                    bottoms.append(jnp.where(live, value, SENTINEL))
                    kept = jnp.where(live, value, 0.0)
                    total = kept if total is None else total + kept
                    count = used if count is None else count + used
                tops, bottoms = sort4(*tops), sort4(*bottoms)
                if upper is None:
                    upper, lower = tops, bottoms
                else:
                    upper = [jnp.maximum(a, b) for a, b in zip(upper, tops[::-1])]
                    lower = [jnp.minimum(a, b) for a, b in zip(lower, bottoms[::-1])]
                    if first + REJECT < HALVES * visits:
                        upper, lower = resort4(*upper), resort4(*lower)
            upper_sum = (upper[0] + upper[1]) + (upper[2] + upper[3])
            lower_sum = (lower[0] + lower[1]) + (lower[2] + lower[3])
            spot = pl.ds(pl.multiple_of(PAD + exp * mine + start + (g // (columns // span)) * 8, 8), 8)
            cpad[spot, cols] = (total - upper_sum - lower_sum) / (count.astype(F32) - 2 * REJECT)
            return carry

        lax.fori_loop(0, (PAD // 8) * (columns // span), group, 0, unroll=2)

    def share(k):
        def at(core):
            return al(PAD + jnp.where(core == 0, mine - PAD - k * PAD, mine + k * PAD))
        rows = pl.ds(at(exp), PAD)
        return remote(cpad.at[rows, :], cpad.at[rows, :], share_send.at[k], share_recv.at[k], other_core)

    def select_block(k):
        select(jnp.where(exp == 0, mine - PAD - k * PAD, k * PAD))

    edge = main // PAD
    co_halo = remote(
        cpad.at[pl.ds(al(PAD + exp * (height - PAD)), PAD), :],
        cpad.at[pl.ds(al((1 - exp) * (PAD + height)), PAD), :],
        co_send, co_recv,
        {"sky": lax.rem(sky + jnp.where(exp == 0, n_sky - 1, 1), n_sky), "exp": 1 - exp},
    )
    select_block(edge)

    @pl.when(has_halo)
    def _():
        co_halo.start()
    share(edge).start()
    for k in range(edge):
        select_block(k)
        share(k).start()

    def filter_rows(first, depth, rows, put_at):
        high, low = parts(cpad[pl.ds(al(first), depth), :])
        smeared = mm(tpsf[put_at:put_at + rows, 0:3 * depth], jnp.concatenate([high, low, high], axis=0))
        partial = jnp.zeros((8, TILE), F32)
        for n, block in enumerate(cols_filter(smeared, wide[psf])):
            squared = block * block
            energy[put_at:put_at + rows, n * TILE:(n + 1) * TILE] = squared
            for r in range(0, rows, 8):
                partial = partial + squared[r:r + 8]
        return partial

    steps = [(db, dx) for db in range(n_band) for dx in range(HALVES)][1:]

    def send_energy(slot, piece):
        db, dx = steps[slot]
        target = lax.rem(band + db, n_band)
        rows = (pl.ds(0, main), pl.ds(main, PAD))[piece]
        return remote(
            energy.at[rows, pl.ds(pl.multiple_of(target * width, TILE), width)],
            land.at[slot, rows, :],
            en_send.at[slot, piece], en_recv.at[slot, piece],
            {"band": target, "exp": exp if dx == 0 else 1 - exp},
        )

    share(0).wait_recv()
    partial = filter_rows(exp * mine + (1 - exp) * PAD, kmain, main, 0)
    for slot in range(len(steps)):
        send_energy(slot, 0).start()
    for k in range(1, edge + 1):
        share(k).wait_recv()
    store_coadd = pltpu.make_async_copy(cpad.at[pl.ds(PAD, height), :], coadd_out.at[0], out_sem.at[0])
    store_coadd.start()

    @pl.when(has_halo)
    def _():
        co_halo.wait_recv()
    partial = partial + filter_rows(exp * (mine + main), kbnd, PAD, main)
    sums[pl.ds(me, 1)] = partial[None]
    if rounds > 3:
        def relay(_, carry):
            hear()
            tell()
            return carry

        lax.fori_loop(0, rounds - 3, relay, 0)
    if rounds > 0:
        hear()

    def send_sum(step):
        return remote(sums.at[me], sums.at[me], sum_send.at[step - 1], sum_recv.at[step - 1], peer_of(step))

    def start_sum(step, carry):
        send_sum(step).start()
        return carry

    lax.fori_loop(1, n_peer, start_sum, 0)
    for slot in range(len(steps)):
        send_energy(slot, 1).start()

    def wait_sum(step, carry):
        send_sum(step).wait_recv()
        return carry

    lax.fori_loop(1, n_peer, wait_sum, 0)
    pixels = height * n_sky * columns

    def inverse(source):
        total = None
        for s in range(n_sky):
            for e in range(HALVES):
                term = sums[(s * n_band + source) * HALVES + e]
                total = term if total is None else total + term
        return 1.0 / (jnp.sum(total, keepdims=True) / pixels + EPSILON)

    inv = [inverse(lax.rem(band + n_band - db, n_band)) for db in range(n_band)]
    for slot in range(len(steps)):
        for piece in range(2):
            send_energy(slot, piece).wait_recv()
    own = energy[:, pl.ds(pl.multiple_of(band * width, TILE), width)] * inv[0]
    far = land[0] * inv[0]
    for db in range(1, n_band):
        own = own + land[db * 2 - 1] * inv[db]
        far = far + land[db * 2] * inv[db]
    for core, value in ((exp, own), (1 - exp, far)):
        det[pl.ds(al(core * mine + (1 - core) * PAD), main), :] = value[0:main]
        det[pl.ds(al(core * (mine + main)), PAD), :] = value[main:]
    store_det = pltpu.make_async_copy(det, det_out, out_sem.at[1])
    store_det.start()

    def drain(c, carry):
        @pl.when(has_after)
        def _():
            halo(0, c).wait_send()

        @pl.when(has_before)
        def _():
            halo(1, c).wait_send()
        return carry

    lax.fori_loop(0, chunks, drain, 0)
    send_far.wait_send()
    send_fmask.wait_send()
    send_taps.wait_send()

    @pl.when(has_halo)
    def _():
        co_halo.wait_send()
    for k in range(edge + 1):
        share(k).wait_send()

    def drain_sum(step, carry):
        send_sum(step).wait_send()
        return carry

    lax.fori_loop(1, n_peer, drain_sum, 0)
    for slot in range(len(steps)):
        for piece in range(2):
            send_energy(slot, piece).wait_send()
    store_coadd.wait()
    store_det.wait()


def hand_on(coadd_in, det_in, coadd_out, det_out, sem):
    copies = [
        pltpu.make_async_copy(coadd_in, coadd_out, sem.at[0]),
        pltpu.make_async_copy(det_in, det_out, sem.at[1]),
    ]
    for copy in copies:
        copy.start()
    for copy in copies:
        copy.wait()


def solution(mesh):
    n_sky, n_band = mesh.shape["sky"], mesh.shape["band"]

    def on_device(images, valid_mask, row_kernel, col_kernel, exp_group, zero_point, psf_row, psf_col):
        _, visits, height, columns = images.shape
        assert height == TILE and mesh.shape["exp"] == HALVES and visits % STACK == 0
        assert visits + 1 <= 16
        width = columns // n_band
        mine = height // HALVES
        main = mine - PAD
        frame = mine + 2 * PAD
        chunks = visits // STACK
        slots = HALVES * visits
        n_peer = n_sky * n_band * HALVES
        n_step = n_band * HALVES - 1
        blocks = mine // PAD
        hbm, anywhere = (pl.BlockSpec(memory_space=space) for space in (pltpu.HBM, pl.ANY))
        dma = pltpu.SemaphoreType.DMA
        shapes = (
            jax.ShapeDtypeStruct((1, height, columns), F32),
            jax.ShapeDtypeStruct((height, width), F32),
        )
        coadd, det = pl.pallas_call(
            functools.partial(kernel, n_sky, n_band),
            out_shape=tuple(pltpu.VMEM(s.shape, s.dtype) for s in shapes),
            in_specs=[hbm] * 8,
            out_specs=(anywhere, anywhere),
            scratch_shapes=[
                pltpu.VMEM((visits, 1, TAPS), F32),
                pltpu.VMEM((visits, 1, TAPS), F32),
                pltpu.VMEM((1, TAPS), F32),
                pltpu.VMEM((1, TAPS), F32),
                pltpu.SMEM(exp_group.shape, jnp.int32),
                pltpu.SMEM(zero_point.shape, F32),
                pltpu.VMEM((slots, frame, columns), BF),
                pltpu.VMEM((slots, mine, columns), jnp.int32),
                pltpu.VMEM((2, 2, 16, 2 * TILE), F32),
                pltpu.VMEM((slots, 2 * main, TILE), BF),
                pltpu.VMEM((slots // STACK, 2 * STACK * PAD, 2 * TILE), BF),
                pltpu.VMEM((mine, 2 * TILE), BF),
                pltpu.VMEM((slots + 1, 2 * TILE, 2 * TILE), BF),
                pltpu.VMEM((slots, mine, columns), F32),
                pltpu.VMEM((height + 2 * PAD, columns), F32),
                pltpu.VMEM((mine, columns), F32),
                pltpu.VMEM((n_step, mine, width), F32),
                pltpu.VMEM((n_peer, 8, TILE), F32),
                pltpu.VMEM((height, width), F32),
                dma((6,)), dma, dma, dma, dma, dma, dma, dma, dma,
                dma((2, chunks)), dma((2, chunks)), dma((blocks,)), dma((blocks,)), dma, dma,
                dma((n_peer - 1,)), dma((n_peer - 1,)), dma((n_step, 2)), dma((n_step, 2)), dma((2,)),
                pltpu.SemaphoreType.REGULAR((2,)),
            ],
            compiler_params=pltpu.CompilerParams(
                collective_id=0, has_side_effects=True, vmem_limit_bytes=48 << 20
            ),
        )(*(
            pltpu.with_memory_space_constraint(array, pltpu.HBM)
            for array in (
                images, valid_mask, jnp.swapaxes(row_kernel, 0, 1), jnp.swapaxes(col_kernel, 0, 1),
                psf_row, psf_col, exp_group, zero_point,
            )
        ))
        return pl.pallas_call(
            hand_on,
            out_shape=shapes,
            in_specs=[anywhere] * 2,
            out_specs=(anywhere, anywhere),
            scratch_shapes=[dma((2,))],
            compiler_params=pltpu.CompilerParams(vmem_limit_bytes=1 << 20),
        )(coadd, det)

    placed = (
        P("band", "exp", ("patch", "sky"), None),
        P("band", "exp", ("patch", "sky"), None),
        P("band", "exp", None),
        P("band", "exp", None),
        P("band", "exp"),
        P("band", None),
        P("band", None),
        P("band", None),
    )
    return jax.shard_map(
        on_device,
        mesh=mesh,
        in_specs=placed,
        out_specs=(P("band", ("patch", "sky"), None), P(("patch", "sky"), "band")),
        check_vma=False,
    )
```

```python
import functools

import jax
import jax.numpy as jnp
from jax import lax
from jax.experimental import pallas as pl
from jax.experimental.pallas import tpu as pltpu
from jax.sharding import PartitionSpec as P

MESH = pl.DeviceIdType.MESH
HALF = 15
REJECT = 4
TAPS = 31
SENTINEL = 1e30
EPSILON = 1e-05
PAD = 16
TILE = 128
HALVES = 2
STACK = 2
AHEAD = 2
BF = jnp.bfloat16
F32 = jnp.float32


def parts(value):
    high = value.astype(BF)
    return high, (value - high.astype(F32)).astype(BF)


def mm(a, b):
    return jnp.dot(a, b, preferred_element_type=F32)


def cols_filter(value, matrix):
    rows, columns = value.shape
    blocks = columns // TILE
    high, low = parts(value)
    zero = jnp.zeros((rows, TILE), BF)
    cut = [slice(n * TILE, (n + 1) * TILE) for n in range(blocks)]
    left = [jnp.concatenate([high[:, at], high[:, at]], axis=1) for at in cut]
    left += [jnp.concatenate([low[:, at], zero], axis=1) for at in cut]
    spread = mm(jnp.concatenate(left, axis=0), matrix)
    spread = [spread[n * rows:(n + 1) * rows] + spread[(blocks + n) * rows:(blocks + n + 1) * rows] for n in range(blocks)]
    joined = [spread[0][:, 0:TILE]]
    for n in range(1, blocks):
        joined.append(spread[n][:, 0:TILE] + spread[n - 1][:, TILE:])
    joined.append(spread[-1][:, TILE:])
    joined = [pltpu.roll(part, TILE // 2, 1) for part in joined]
    first = lax.broadcasted_iota(jnp.int32, (rows, TILE), 1) < TILE // 2
    return [jnp.where(first, joined[n], joined[n + 1]) for n in range(blocks)]


def swap(a, b):
    return jnp.minimum(a, b), jnp.maximum(a, b)


def sort4(a, b, c, d):
    a, b = swap(a, b)
    c, d = swap(c, d)
    a, c = swap(a, c)
    b, d = swap(b, d)
    b, c = swap(b, c)
    return [a, b, c, d]


def resort4(a, b, c, d):
    a, c = swap(a, c)
    b, d = swap(b, d)
    a, b = swap(a, b)
    c, d = swap(c, d)
    return [a, b, c, d]


def kernel(
    n_sky, n_band,
    img, mask, rk_in, ck_in, pr_in, pc_in, eg_in, zp_in,
    coadd_out, det_out,
    rk, ck, pr, pc, eg, zp, x, msk, taps, trow, tedge, tpsf, wide, vals, lists, counts, cpad, energy, land, sums,
    arg_sem, img_sem, mask_sem, tap_send, tap_recv, far_send, far_recv, fmask_send, fmask_recv,
    halo_send, halo_recv, share_send, share_recv, co_send, co_recv, sum_send, sum_recv, en_send, en_recv, out_sem, token,
):
    visits, height, columns = img.shape[1:]
    mine = height // HALVES
    main = mine - PAD
    frame = mine + 2 * PAD
    kmain, kbnd = main + 2 * PAD, 3 * PAD
    width = columns // n_band
    chunks = visits // STACK
    sky, band, exp = lax.axis_index("sky"), lax.axis_index("band"), lax.axis_index("exp")
    has_before, has_after = sky > 0, sky < n_sky - 1
    has_halo = jnp.where(exp == 0, sky, n_sky - 1 - sky) > 0
    n_peer = n_sky * n_band * HALVES
    me = (sky * n_band + band) * HALVES + exp

    def peer_of(step):
        peer = lax.rem(me + step, n_peer)
        chip = peer // HALVES
        return {"sky": chip // n_band, "band": lax.rem(chip, n_band), "exp": lax.rem(peer, HALVES)}

    other_core = {"exp": 1 - exp}

    def remote(source, target, send, recv, device):
        return pltpu.make_async_remote_copy(
            src_ref=source, dst_ref=target, send_sem=send, recv_sem=recv, device_id=device, device_id_type=MESH,
        )

    def al(value):
        return pl.multiple_of(value, PAD)

    barrier = pltpu.get_barrier_semaphore()

    def beside(side):
        return lax.rem(sky + (1, n_sky - 1)[side], n_sky)

    exists = (has_after, has_before)
    for side in range(2):
        @pl.when(exists[side])
        def _():
            for core in range(HALVES):
                pl.semaphore_signal(barrier, inc=1, device_id={"sky": beside(side), "exp": core}, device_id_type=MESH)
    pl.semaphore_signal(barrier, inc=1, device_id=other_core, device_id_type=MESH)
    for db in range(1, n_band):
        for core in range(HALVES):
            pl.semaphore_signal(
                barrier, inc=1, device_id={"band": lax.rem(band + db, n_band), "exp": core}, device_id_type=MESH
            )

    small = [
        pltpu.make_async_copy(source, target, arg_sem.at[k])
        for k, (source, target) in enumerate(
            ((eg_in, eg), (zp_in, zp), (ck_in, ck), (pc_in, pc), (rk_in, rk), (pr_in, pr))
        )
    ]
    for copy in small:
        copy.start()

    load_img = pltpu.make_async_copy(
        img.at[0, :, pl.ds(al(exp * (mine - PAD)), kmain), :],
        x.at[pl.ds(0, visits), pl.ds(al((1 - exp) * PAD), kmain), :], img_sem,
    )
    load_img.start()
    load_mask = pltpu.make_async_copy(
        mask.at[0, :, pl.ds(al(exp * mine), mine), :], msk.at[pl.ds(0, visits)], mask_sem
    )
    load_mask.start()
    taps[0] = jnp.zeros(taps.shape[1:], F32)
    for copy in small:
        copy.wait()
    for v in range(visits):
        taps[0, 0, v:v + 1, 0:TAPS] = rk[v]
    taps[0, 0, visits:visits + 1, 0:TAPS] = pr[...]
    for v in range(visits):
        taps[0, 1, v:v + 1, 0:TAPS] = ck[v] * zp[0, eg[0, v]]
    taps[0, 1, visits:visits + 1, 0:TAPS] = pc[...]
    at_row = lax.broadcasted_iota(jnp.int32, (TILE, TILE), 0)
    at_col = lax.broadcasted_iota(jnp.int32, (TILE, TILE), 1)
    flip = (at_col == TILE // 2 + HALF - at_row).astype(F32)
    taps[0, 1, :, 0:TILE] = jnp.dot(taps[0, 1, :, 0:TILE], flip, preferred_element_type=F32, precision=lax.Precision.HIGHEST)
    greeted = sum(jnp.where(there, HALVES, 0) for there in exists)
    pl.semaphore_wait(barrier, greeted + 1 + HALVES * (n_band - 1))

    rounds = n_sky - 1

    def tell():
        for side in range(2):
            @pl.when(exists[side])
            def _():
                pl.semaphore_signal(token.at[side], inc=1, device_id={"sky": beside(side)}, device_id_type=MESH)

    def hear():
        for side in range(2):
            @pl.when(exists[1 - side])
            def _():
                pl.semaphore_wait(token.at[side], 1)

    def halo(side, c):
        start, land_at = ((height - PAD, 0), (0, PAD + mine))[side]
        slot = jnp.where(exp == side, 0, visits) + c * STACK
        return remote(
            img.at[0, pl.ds(c * STACK, STACK), pl.ds(start, PAD), :],
            x.at[pl.ds(slot, STACK), pl.ds(land_at, PAD), :],
            halo_send.at[side, c], halo_recv.at[jnp.where(exp == side, 0, 1), c],
            {"sky": beside(side), "exp": side},
        )

    def start_halo(c, carry):
        @pl.when(has_after)
        def _():
            halo(0, c).start()

        @pl.when(has_before)
        def _():
            halo(1, c).start()
        return carry

    lax.fori_loop(0, chunks, start_halo, 0)

    send_far = remote(
        img.at[0, :, pl.ds(al((1 - exp) * (mine - PAD)), kmain), :],
        x.at[pl.ds(visits, visits), pl.ds(al(exp * PAD), kmain), :],
        far_send, far_recv, other_core,
    )
    send_far.start()
    def send_mask(k):
        far = 1 - exp
        start, rows = ((far * main, PAD), ((1 - far) * PAD, main))[k]
        return remote(
            mask.at[0, :, pl.ds(al(far * mine + start), rows), :],
            msk.at[pl.ds(visits, visits), pl.ds(al(start), rows), :],
            fmask_send.at[k], fmask_recv.at[k], other_core,
        )

    def take_mask(k):
        start, rows = ((exp * main, PAD), ((1 - exp) * PAD, main))[k]
        piece = msk.at[pl.ds(visits, visits), pl.ds(al(start), rows), :]
        return remote(piece, piece, fmask_send.at[k], fmask_recv.at[k], other_core)

    send_mask(0).start()
    tell()

    send_taps = remote(taps.at[0], taps.at[1], tap_send, tap_recv, other_core)
    send_taps.start()
    send_mask(1).start()

    @pl.when(jnp.logical_not(has_halo))
    def _():
        x[:, pl.ds(al(exp * (PAD + mine)), PAD), :] = jnp.zeros((HALVES * visits, PAD, columns), BF)
        cpad[pl.ds(al(exp * (PAD + height)), PAD), :] = jnp.zeros((PAD, columns), F32)

    upward = (at_col > at_row).astype(F32).astype(BF)

    def slanted(origin, v, rows, lanes, shift):
        line = jnp.broadcast_to(taps[origin, 0, v:v + 1, 0:lanes], (rows, lanes))
        return pltpu.roll(line, shift, 1, stride=1, stride_axis=0)

    def build_wide(origin, v, slot):
        line = jnp.broadcast_to(taps[origin, 1, v:v + 1, 0:TILE], (TILE, TILE))
        line = pltpu.roll(line, 0, 1, stride=1, stride_axis=0)
        for n, part in enumerate(parts(line)):
            here = part * upward
            wide[slot, n * TILE:(n + 1) * TILE, 0:TILE] = here
            wide[slot, n * TILE:(n + 1) * TILE, TILE:] = part - here

    def build(origin, v):
        slot = origin * visits + v
        for n, part in enumerate(parts(slanted(origin, v, main, TILE, 1))):
            trow[slot, n * main:(n + 1) * main, :] = part
        group, j = v // STACK, origin * STACK + v % STACK
        for n, part in enumerate(parts(slanted(origin, v, PAD, 2 * TILE, j * kbnd + 1))):
            tedge[group, (n * REJECT + j) * PAD:(n * REJECT + j + 1) * PAD, :] = part
        build_wide(origin, v, slot)

    def smear(slot):
        both = mm(trow[slot, :, 0:kmain], x[slot, pl.ds(al((1 - exp) * PAD), kmain), :])
        return both[0:main] + both[main:]

    def put(slot, start, rows, value):
        for n, block in enumerate(cols_filter(value, wide[slot])):
            vals[slot, pl.ds(al(start), rows), n * TILE:(n + 1) * TILE] = block

    def convolve(origin):
        waiting = []
        for v in range(visits):
            build(origin, v)
            slot = origin * visits + v
            waiting.append((slot, smear(slot)))
            if len(waiting) > AHEAD:
                done, value = waiting.pop(0)
                put(done, (1 - exp) * PAD, main, value)
        for done, value in waiting:
            put(done, (1 - exp) * PAD, main, value)

    load_img.wait()
    convolve(0)
    if rounds > 1:
        hear()
        tell()
    send_taps.wait_recv()
    send_far.wait_recv()
    convolve(1)
    if rounds > 2:
        hear()
        tell()

    psf = HALVES * visits
    build_wide(0, visits, psf)
    for rows, depth, at in ((main, kmain, 0), (PAD, kbnd, main)):
        pieces = [parts(slanted(0, visits, rows, 2 * TILE, j * depth + 1))[int(j == 2)] for j in range(3)]
        tpsf[at:at + rows, :] = pieces[0] + pieces[1] + pieces[2]

    edge_rows_of_x = pl.ds(al(exp * main), kbnd)

    def halo_wait(source, c):
        land_at = al(exp * (PAD + mine))
        piece = x.at[pl.ds(source * visits + c * STACK, STACK), pl.ds(land_at, PAD), :]
        return remote(piece, piece, halo_send.at[0, c], halo_recv.at[source, c], other_core)

    load_mask.wait()
    take_mask(0).wait_recv()

    def gather(values, masks, total, count):
        tops, bottoms = [], []
        for value, used in zip(values, masks):
            live = used == 1
            tops.append(jnp.where(live, value, -SENTINEL))
            bottoms.append(jnp.where(live, value, SENTINEL))
            kept = jnp.where(live, value, 0.0)
            total = kept if total is None else total + kept
            count = used if count is None else count + used
        return sort4(*tops), sort4(*bottoms), total, count

    def merge(upper, lower, tops, bottoms):
        upper = [jnp.maximum(a, b) for a, b in zip(upper, tops[::-1])]
        lower = [jnp.minimum(a, b) for a, b in zip(lower, bottoms[::-1])]
        return upper, lower

    def trimmed(upper, lower, total, count):
        upper_sum = (upper[0] + upper[1]) + (upper[2] + upper[3])
        lower_sum = (lower[0] + lower[1]) + (lower[2] + lower[3])
        return (total - upper_sum - lower_sum) / (count.astype(F32) - 2 * REJECT)

    edge_rows = pl.ds(al(exp * main), PAD)
    edge_spot = pl.ds(al(PAD + exp * (mine + main)), PAD)
    for c in range(chunks):
        @pl.when(has_halo)
        def _():
            for source in range(HALVES):
                halo_wait(source, c).wait_recv()
        slots = [source * visits + c * STACK + u for source in range(HALVES) for u in range(STACK)]
        stacked = jnp.concatenate([x[slot, edge_rows_of_x, :] for slot in slots], axis=0)
        both = mm(tedge[c, :, 0:REJECT * kbnd], stacked)
        smeared = both[0:REJECT * PAD] + both[REJECT * PAD:]
        found = [cols_filter(smeared[u * PAD:(u + 1) * PAD], wide[slot]) for u, slot in enumerate(slots)]
        for n in range(columns // TILE):
            cols = slice(n * TILE, (n + 1) * TILE)
            total, count = (None, None) if c == 0 else (lists[2 * REJECT, :, cols], counts[:, cols])
            tops, bottoms, total, count = gather(
                [blocks[n] for blocks in found], [msk[slot, edge_rows, cols] for slot in slots], total, count
            )
            upper, lower = tops, bottoms
            if c > 0:
                upper, lower = merge(
                    [lists[k, :, cols] for k in range(REJECT)], [lists[REJECT + k, :, cols] for k in range(REJECT)],
                    tops, bottoms,
                )
            if c == chunks - 1:
                cpad[edge_spot, cols] = trimmed(upper, lower, total, count)
            else:
                if c > 0:
                    upper, lower = resort4(*upper), resort4(*lower)
                for k, item in enumerate(upper + lower + [total]):
                    lists[k, :, cols] = item
                counts[:, cols] = count

    def select(start):
        span = 2 * TILE

        def group(g, carry):
            rows = pl.ds(pl.multiple_of(start + (g // (columns // span)) * 8, 8), 8)
            cols = pl.ds(pl.multiple_of(lax.rem(g, columns // span) * span, span), span)
            upper, lower, total, count = None, None, None, None
            for first in range(0, HALVES * visits, REJECT):
                slots = range(first, first + REJECT)
                tops, bottoms, total, count = gather(
                    [vals[v, rows, cols] for v in slots], [msk[v, rows, cols] for v in slots], total, count
                )
                if upper is None:
                    upper, lower = tops, bottoms
                else:
                    upper, lower = merge(upper, lower, tops, bottoms)
                    if first + REJECT < HALVES * visits:
                        upper, lower = resort4(*upper), resort4(*lower)
            spot = pl.ds(pl.multiple_of(PAD + exp * mine + start + (g // (columns // span)) * 8, 8), 8)
            cpad[spot, cols] = trimmed(upper, lower, total, count)
            return carry

        lax.fori_loop(0, (PAD // 8) * (columns // span), group, 0, unroll=2)

    def share(k):
        def at(core):
            return al(PAD + jnp.where(core == 0, mine - PAD - k * PAD, mine + k * PAD))
        rows = pl.ds(at(exp), PAD)
        return remote(cpad.at[rows, :], cpad.at[rows, :], share_send.at[k], share_recv.at[k], other_core)

    def select_block(k):
        select(jnp.where(exp == 0, mine - PAD - k * PAD, k * PAD))

    edge = main // PAD
    co_halo = remote(
        cpad.at[pl.ds(al(PAD + exp * (height - PAD)), PAD), :],
        cpad.at[pl.ds(al((1 - exp) * (PAD + height)), PAD), :],
        co_send, co_recv,
        {"sky": lax.rem(sky + jnp.where(exp == 0, n_sky - 1, 1), n_sky), "exp": 1 - exp},
    )

    @pl.when(has_halo)
    def _():
        co_halo.start()
    share(edge).start()
    take_mask(1).wait_recv()
    for k in range(edge):
        select_block(k)
        share(k).start()

    def filter_rows(first, depth, rows, put_at):
        high, low = parts(cpad[pl.ds(al(first), depth), :])
        smeared = mm(tpsf[put_at:put_at + rows, 0:3 * depth], jnp.concatenate([high, low, high], axis=0))
        partial = jnp.zeros((8, TILE), F32)
        for n, block in enumerate(cols_filter(smeared, wide[psf])):
            squared = block * block
            energy[put_at:put_at + rows, n * TILE:(n + 1) * TILE] = squared
            for r in range(0, rows, 8):
                partial = partial + squared[r:r + 8]
        return partial

    steps = [(db, dx) for db in range(n_band) for dx in range(HALVES)][1:]

    def send_energy(slot, piece):
        db, dx = steps[slot]
        target = lax.rem(band + db, n_band)
        rows = (pl.ds(0, main), pl.ds(main, PAD))[piece]
        return remote(
            energy.at[rows, pl.ds(pl.multiple_of(target * width, TILE), width)],
            land.at[slot, rows, :],
            en_send.at[slot, piece], en_recv.at[slot, piece],
            {"band": target, "exp": exp if dx == 0 else 1 - exp},
        )

    share(0).wait_recv()
    partial = filter_rows(exp * mine + (1 - exp) * PAD, kmain, main, 0)
    for slot in range(len(steps)):
        send_energy(slot, 0).start()
    for k in range(1, edge + 1):
        share(k).wait_recv()
    store_coadd = pltpu.make_async_copy(cpad.at[pl.ds(PAD, height), :], coadd_out.at[0], out_sem)
    store_coadd.start()

    @pl.when(has_halo)
    def _():
        co_halo.wait_recv()
    partial = partial + filter_rows(exp * (mine + main), kbnd, PAD, main)
    sums[pl.ds(me, 1)] = jnp.sum(partial, axis=0, keepdims=True)[None]
    if rounds > 3:
        def relay(_, carry):
            hear()
            tell()
            return carry

        lax.fori_loop(0, rounds - 3, relay, 0)
    if rounds > 0:
        hear()

    def send_sum(step):
        return remote(sums.at[me], sums.at[me], sum_send.at[step - 1], sum_recv.at[step - 1], peer_of(step))

    def start_sum(step, carry):
        send_sum(step).start()
        return carry

    lax.fori_loop(1, n_peer, start_sum, 0, unroll=n_peer <= 16)
    for slot in range(len(steps)):
        send_energy(slot, 1).start()

    def wait_sum(step, carry):
        send_sum(step).wait_recv()
        return carry

    lax.fori_loop(1, n_peer, wait_sum, 0, unroll=n_peer <= 16)
    pixels = height * n_sky * columns

    def inverse(source):
        total = None
        for s in range(n_sky):
            for e in range(HALVES):
                term = sums[(s * n_band + source) * HALVES + e]
                total = term if total is None else total + term
        return 1.0 / (jnp.sum(total, keepdims=True) / pixels + EPSILON)

    inv = [inverse(lax.rem(band + n_band - db, n_band)) for db in range(n_band)]
    for slot in range(len(steps)):
        for piece in range(2):
            send_energy(slot, piece).wait_recv()
    own = energy[:, pl.ds(pl.multiple_of(band * width, TILE), width)] * inv[0]
    far = land[0] * inv[0]
    for db in range(1, n_band):
        own = own + land[db * 2 - 1] * inv[db]
        far = far + land[db * 2] * inv[db]
    for core, value in ((exp, own), (1 - exp, far)):
        det_out[pl.ds(al(core * mine + (1 - core) * PAD), main), :] = value[0:main]
        det_out[pl.ds(al(core * (mine + main)), PAD), :] = value[main:]

    def drain(c, carry):
        @pl.when(has_after)
        def _():
            halo(0, c).wait_send()

        @pl.when(has_before)
        def _():
            halo(1, c).wait_send()
        return carry

    lax.fori_loop(0, chunks, drain, 0)
    send_far.wait_send()
    for k in range(2):
        send_mask(k).wait_send()
    send_taps.wait_send()

    @pl.when(has_halo)
    def _():
        co_halo.wait_send()
    for k in range(edge + 1):
        share(k).wait_send()

    def drain_sum(step, carry):
        send_sum(step).wait_send()
        return carry

    lax.fori_loop(1, n_peer, drain_sum, 0, unroll=n_peer <= 16)
    for slot in range(len(steps)):
        for piece in range(2):
            send_energy(slot, piece).wait_send()
    store_coadd.wait()


def hand_on(coadd_in, det_in, coadd_out, det_out, sem):
    copies = [
        pltpu.make_async_copy(coadd_in, coadd_out, sem.at[0]),
        pltpu.make_async_copy(det_in, det_out, sem.at[1]),
    ]
    for copy in copies:
        copy.start()
    for copy in copies:
        copy.wait()


def solution(mesh):
    n_sky, n_band = mesh.shape["sky"], mesh.shape["band"]

    def on_device(images, valid_mask, row_kernel, col_kernel, exp_group, zero_point, psf_row, psf_col):
        _, visits, height, columns = images.shape
        assert height == TILE and mesh.shape["exp"] == HALVES and visits % STACK == 0
        assert visits + 1 <= 16 and STACK * HALVES == REJECT
        width = columns // n_band
        mine = height // HALVES
        main = mine - PAD
        frame = mine + 2 * PAD
        chunks = visits // STACK
        slots = HALVES * visits
        n_peer = n_sky * n_band * HALVES
        n_step = n_band * HALVES - 1
        blocks = mine // PAD
        hbm, anywhere = (pl.BlockSpec(memory_space=space) for space in (pltpu.HBM, pl.ANY))
        dma = pltpu.SemaphoreType.DMA
        shapes = (
            jax.ShapeDtypeStruct((1, height, columns), F32),
            jax.ShapeDtypeStruct((height, width), F32),
        )
        coadd, det = pl.pallas_call(
            functools.partial(kernel, n_sky, n_band),
            out_shape=tuple(pltpu.VMEM(s.shape, s.dtype) for s in shapes),
            in_specs=[hbm] * 8,
            out_specs=(anywhere, pl.BlockSpec(memory_space=pltpu.VMEM)),
            scratch_shapes=[
                pltpu.VMEM((visits, 1, TAPS), F32),
                pltpu.VMEM((visits, 1, TAPS), F32),
                pltpu.VMEM((1, TAPS), F32),
                pltpu.VMEM((1, TAPS), F32),
                pltpu.SMEM(exp_group.shape, jnp.int32),
                pltpu.SMEM(zero_point.shape, F32),
                pltpu.VMEM((slots, frame, columns), BF),
                pltpu.VMEM((slots, mine, columns), jnp.int32),
                pltpu.VMEM((2, 2, 16, 2 * TILE), F32),
                pltpu.VMEM((slots, 2 * main, TILE), BF),
                pltpu.VMEM((chunks, 2 * REJECT * PAD, 2 * TILE), BF),
                pltpu.VMEM((mine, 2 * TILE), BF),
                pltpu.VMEM((slots + 1, 2 * TILE, 2 * TILE), BF),
                pltpu.VMEM((slots, mine, columns), F32),
                pltpu.VMEM((2 * REJECT + 1, PAD, columns), F32),
                pltpu.VMEM((PAD, columns), jnp.int32),
                pltpu.VMEM((height + 2 * PAD, columns), F32),
                pltpu.VMEM((mine, columns), F32),
                pltpu.VMEM((n_step, mine, width), F32),
                pltpu.VMEM((n_peer, 1, TILE), F32),
                dma((6,)), dma, dma, dma, dma, dma, dma, dma((2,)), dma((2,)),
                dma((2, chunks)), dma((2, chunks)), dma((blocks,)), dma((blocks,)), dma, dma,
                dma((n_peer - 1,)), dma((n_peer - 1,)), dma((n_step, 2)), dma((n_step, 2)), dma,
                pltpu.SemaphoreType.REGULAR((2,)),
            ],
            compiler_params=pltpu.CompilerParams(
                collective_id=0, has_side_effects=True, vmem_limit_bytes=48 << 20
            ),
        )(*(
            pltpu.with_memory_space_constraint(array, pltpu.HBM)
            for array in (
                images, valid_mask, jnp.swapaxes(row_kernel, 0, 1), jnp.swapaxes(col_kernel, 0, 1),
                psf_row, psf_col, exp_group, zero_point,
            )
        ))
        return pl.pallas_call(
            hand_on,
            out_shape=shapes,
            in_specs=[anywhere] * 2,
            out_specs=(anywhere, anywhere),
            scratch_shapes=[dma((2,))],
            compiler_params=pltpu.CompilerParams(vmem_limit_bytes=1 << 20),
        )(coadd, det)

    placed = (
        P("band", "exp", ("patch", "sky"), None),
        P("band", "exp", ("patch", "sky"), None),
        P("band", "exp", None),
        P("band", "exp", None),
        P("band", "exp"),
        P("band", None),
        P("band", None),
        P("band", None),
    )
    return jax.shard_map(
        on_device,
        mesh=mesh,
        in_specs=placed,
        out_specs=(P("band", ("patch", "sky"), None), P(("patch", "sky"), "band")),
        check_vma=False,
    )
```

```python
import functools

import jax
import jax.numpy as jnp
from jax import lax
from jax.experimental import pallas as pl
from jax.experimental.pallas import tpu as pltpu
from jax.sharding import PartitionSpec as P

MESH = pl.DeviceIdType.MESH
HALF = 15
REJECT = 4
TAPS = 31
SENTINEL = 1e30
EPSILON = 1e-05
PAD = 16
TILE = 128
HALVES = 2
STACK = 2
AHEAD = 2
FAR = 2
BF = jnp.bfloat16
F32 = jnp.float32


def parts(value):
    high = value.astype(BF)
    return high, (value - high.astype(F32)).astype(BF)


def mm(a, b):
    return jnp.dot(a, b, preferred_element_type=F32)


def cols_filter(value, matrix):
    rows, columns = value.shape
    blocks = columns // TILE
    high, low = parts(value)
    zero = jnp.zeros((rows, TILE), BF)
    cut = [slice(n * TILE, (n + 1) * TILE) for n in range(blocks)]
    left = [jnp.concatenate([high[:, at], high[:, at]], axis=1) for at in cut]
    left += [jnp.concatenate([low[:, at], zero], axis=1) for at in cut]
    spread = mm(jnp.concatenate(left, axis=0), matrix)
    spread = [spread[n * rows:(n + 1) * rows] + spread[(blocks + n) * rows:(blocks + n + 1) * rows] for n in range(blocks)]
    joined = [spread[0][:, 0:TILE]]
    for n in range(1, blocks):
        joined.append(spread[n][:, 0:TILE] + spread[n - 1][:, TILE:])
    joined.append(spread[-1][:, TILE:])
    joined = [pltpu.roll(part, TILE // 2, 1) for part in joined]
    first = lax.broadcasted_iota(jnp.int32, (rows, TILE), 1) < TILE // 2
    return [jnp.where(first, joined[n], joined[n + 1]) for n in range(blocks)]


def swap(a, b):
    return jnp.minimum(a, b), jnp.maximum(a, b)


def sort4(a, b, c, d):
    a, b = swap(a, b)
    c, d = swap(c, d)
    a, c = swap(a, c)
    b, d = swap(b, d)
    b, c = swap(b, c)
    return [a, b, c, d]


def resort4(a, b, c, d):
    a, c = swap(a, c)
    b, d = swap(b, d)
    a, b = swap(a, b)
    c, d = swap(c, d)
    return [a, b, c, d]


def kernel(
    n_sky, n_band,
    img, mask, rk_in, ck_in, pr_in, pc_in, eg_in, zp_in,
    coadd_out, energy, land, sums,
    rk, ck, pr, pc, eg, zp, x, msk, taps, trow, tedge, tpsf, wide, vals, lists, counts, squares, cpad,
    arg_sem, img_sem, mask_sem, tap_send, tap_recv, far_send, far_recv, fmask_send, fmask_recv,
    halo_send, halo_recv, share_send, share_recv, co_send, co_recv, sum_send, sum_recv, en_send, en_recv, out_sem, token,
):
    visits, height, columns = img.shape[1:]
    mine = height // HALVES
    main = mine - PAD
    frame = mine + 2 * PAD
    kmain, kbnd = main + 2 * PAD, 3 * PAD
    width = columns // n_band
    chunks = visits // STACK
    sky, band, exp = lax.axis_index("sky"), lax.axis_index("band"), lax.axis_index("exp")
    has_before, has_after = sky > 0, sky < n_sky - 1
    has_halo = jnp.where(exp == 0, sky, n_sky - 1 - sky) > 0
    n_peer = n_sky * n_band * HALVES
    me = (sky * n_band + band) * HALVES + exp

    def peer_of(step):
        peer = lax.rem(me + step, n_peer)
        chip = peer // HALVES
        return {"sky": chip // n_band, "band": lax.rem(chip, n_band), "exp": lax.rem(peer, HALVES)}

    other_core = {"exp": 1 - exp}

    def remote(source, target, send, recv, device):
        return pltpu.make_async_remote_copy(
            src_ref=source, dst_ref=target, send_sem=send, recv_sem=recv, device_id=device, device_id_type=MESH,
        )

    def al(value):
        return pl.multiple_of(value, PAD)

    barrier = pltpu.get_barrier_semaphore()

    def beside(side):
        return lax.rem(sky + (1, n_sky - 1)[side], n_sky)

    exists = (has_after, has_before)
    for side in range(2):
        @pl.when(exists[side])
        def _():
            for core in range(HALVES):
                pl.semaphore_signal(barrier, inc=1, device_id={"sky": beside(side), "exp": core}, device_id_type=MESH)
    pl.semaphore_signal(barrier, inc=1, device_id=other_core, device_id_type=MESH)
    for db in range(1, n_band):
        for core in range(HALVES):
            pl.semaphore_signal(
                barrier, inc=1, device_id={"band": lax.rem(band + db, n_band), "exp": core}, device_id_type=MESH
            )

    small = [
        pltpu.make_async_copy(source, target, arg_sem.at[k])
        for k, (source, target) in enumerate(
            ((eg_in, eg), (zp_in, zp), (ck_in, ck), (pc_in, pc), (rk_in, rk), (pr_in, pr))
        )
    ]
    for copy in small:
        copy.start()

    load_img = pltpu.make_async_copy(
        img.at[0, :, pl.ds(al(exp * (mine - PAD)), kmain), :],
        x.at[pl.ds(0, visits), pl.ds(al((1 - exp) * PAD), kmain), :], img_sem,
    )
    load_img.start()
    load_mask = pltpu.make_async_copy(
        mask.at[0, :, pl.ds(al(exp * mine), mine), :], msk.at[pl.ds(0, visits)], mask_sem
    )
    load_mask.start()
    taps[0] = jnp.zeros(taps.shape[1:], F32)
    for copy in small:
        copy.wait()
    for v in range(visits):
        taps[0, 0, v:v + 1, 0:TAPS] = rk[v]
    taps[0, 0, visits:visits + 1, 0:TAPS] = pr[...]
    for v in range(visits):
        taps[0, 1, v:v + 1, 0:TAPS] = ck[v] * zp[0, eg[0, v]]
    taps[0, 1, visits:visits + 1, 0:TAPS] = pc[...]
    at_row = lax.broadcasted_iota(jnp.int32, (TILE, TILE), 0)
    at_col = lax.broadcasted_iota(jnp.int32, (TILE, TILE), 1)
    flip = (at_col == TILE // 2 + HALF - at_row).astype(F32)
    taps[0, 1, :, 0:TILE] = jnp.dot(taps[0, 1, :, 0:TILE], flip, preferred_element_type=F32, precision=lax.Precision.HIGHEST)
    greeted = sum(jnp.where(there, HALVES, 0) for there in exists)
    pl.semaphore_wait(barrier, greeted + 1 + HALVES * (n_band - 1))

    rounds = n_sky - 1

    def tell():
        for side in range(2):
            @pl.when(exists[side])
            def _():
                pl.semaphore_signal(token.at[side], inc=1, device_id={"sky": beside(side)}, device_id_type=MESH)

    def hear():
        for side in range(2):
            @pl.when(exists[1 - side])
            def _():
                pl.semaphore_wait(token.at[side], 1)

    def halo(side, c):
        start, land_at = ((height - PAD, 0), (0, PAD + mine))[side]
        slot = jnp.where(exp == side, 0, visits) + c * STACK
        return remote(
            img.at[0, pl.ds(c * STACK, STACK), pl.ds(start, PAD), :],
            x.at[pl.ds(slot, STACK), pl.ds(land_at, PAD), :],
            halo_send.at[side, c], halo_recv.at[jnp.where(exp == side, 0, 1), c],
            {"sky": beside(side), "exp": side},
        )

    def start_halo(c, carry):
        @pl.when(has_after)
        def _():
            halo(0, c).start()

        @pl.when(has_before)
        def _():
            halo(1, c).start()
        return carry

    lax.fori_loop(0, chunks, start_halo, 0)

    def send_far(k):
        some = visits // FAR
        return remote(
            img.at[0, pl.ds(k * some, some), pl.ds(al((1 - exp) * (mine - PAD)), kmain), :],
            x.at[pl.ds(visits + k * some, some), pl.ds(al(exp * PAD), kmain), :],
            far_send.at[k], far_recv.at[k], other_core,
        )

    def take_far(k):
        some = visits // FAR
        piece = x.at[pl.ds(visits + k * some, some), pl.ds(al((1 - exp) * PAD), kmain), :]
        return remote(piece, piece, far_send.at[k], far_recv.at[k], other_core)

    for k in range(FAR):
        send_far(k).start()
    def send_mask(k):
        far = 1 - exp
        start, rows = ((far * main, PAD), ((1 - far) * PAD, main))[k]
        return remote(
            mask.at[0, :, pl.ds(al(far * mine + start), rows), :],
            msk.at[pl.ds(visits, visits), pl.ds(al(start), rows), :],
            fmask_send.at[k], fmask_recv.at[k], other_core,
        )

    def take_mask(k):
        start, rows = ((exp * main, PAD), ((1 - exp) * PAD, main))[k]
        piece = msk.at[pl.ds(visits, visits), pl.ds(al(start), rows), :]
        return remote(piece, piece, fmask_send.at[k], fmask_recv.at[k], other_core)

    send_mask(0).start()
    tell()

    send_taps = remote(taps.at[0], taps.at[1], tap_send, tap_recv, other_core)
    send_taps.start()
    send_mask(1).start()

    @pl.when(jnp.logical_not(has_halo))
    def _():
        x[:, pl.ds(al(exp * (PAD + mine)), PAD), :] = jnp.zeros((HALVES * visits, PAD, columns), BF)
        cpad[pl.ds(al(exp * (PAD + height)), PAD), :] = jnp.zeros((PAD, columns), F32)

    upward = (at_col > at_row).astype(F32).astype(BF)

    def slanted(origin, v, rows, lanes, shift):
        line = jnp.broadcast_to(taps[origin, 0, v:v + 1, 0:lanes], (rows, lanes))
        return pltpu.roll(line, shift, 1, stride=1, stride_axis=0)

    def build_wide(origin, v, slot):
        line = jnp.broadcast_to(taps[origin, 1, v:v + 1, 0:TILE], (TILE, TILE))
        line = pltpu.roll(line, 0, 1, stride=1, stride_axis=0)
        for n, part in enumerate(parts(line)):
            here = part * upward
            wide[slot, n * TILE:(n + 1) * TILE, 0:TILE] = here
            wide[slot, n * TILE:(n + 1) * TILE, TILE:] = part - here

    def build(origin, v):
        slot = origin * visits + v
        for n, part in enumerate(parts(slanted(origin, v, main, TILE, 1))):
            trow[slot, n * main:(n + 1) * main, :] = part
        group, j = v // STACK, origin * STACK + v % STACK
        for n, part in enumerate(parts(slanted(origin, v, PAD, 2 * TILE, j * kbnd + 1))):
            tedge[group, (n * REJECT + j) * PAD:(n * REJECT + j + 1) * PAD, :] = part
        build_wide(origin, v, slot)

    def smear(slot):
        both = mm(trow[slot, :, 0:kmain], x[slot, pl.ds(al((1 - exp) * PAD), kmain), :])
        return both[0:main] + both[main:]

    def put(slot, start, rows, value):
        for n, block in enumerate(cols_filter(value, wide[slot])):
            vals[slot, pl.ds(al(start), rows), n * TILE:(n + 1) * TILE] = block

    def convolve(origin):
        waiting = []
        for v in range(visits):
            if origin and v % (visits // FAR) == 0:
                take_far(v // (visits // FAR)).wait_recv()
            build(origin, v)
            slot = origin * visits + v
            waiting.append((slot, smear(slot)))
            if len(waiting) > AHEAD:
                done, value = waiting.pop(0)
                put(done, (1 - exp) * PAD, main, value)
        for done, value in waiting:
            put(done, (1 - exp) * PAD, main, value)

    load_img.wait()
    convolve(0)
    if rounds > 1:
        hear()
        tell()
    send_taps.wait_recv()
    convolve(1)
    if rounds > 2:
        hear()
        tell()

    psf = HALVES * visits
    build_wide(0, visits, psf)
    for rows, depth, at in ((main, kmain, 0), (PAD, kbnd, main)):
        pieces = [parts(slanted(0, visits, rows, 2 * TILE, j * depth + 1))[int(j == 2)] for j in range(3)]
        tpsf[at:at + rows, :] = pieces[0] + pieces[1] + pieces[2]

    edge_rows_of_x = pl.ds(al(exp * main), kbnd)

    def halo_wait(source, c):
        land_at = al(exp * (PAD + mine))
        piece = x.at[pl.ds(source * visits + c * STACK, STACK), pl.ds(land_at, PAD), :]
        return remote(piece, piece, halo_send.at[0, c], halo_recv.at[source, c], other_core)

    load_mask.wait()
    take_mask(0).wait_recv()

    def gather(values, masks, total, count):
        tops, bottoms = [], []
        for value, used in zip(values, masks):
            live = used == 1
            tops.append(jnp.where(live, value, -SENTINEL))
            bottoms.append(jnp.where(live, value, SENTINEL))
            kept = jnp.where(live, value, 0.0)
            total = kept if total is None else total + kept
            count = used if count is None else count + used
        return sort4(*tops), sort4(*bottoms), total, count

    def merge(upper, lower, tops, bottoms):
        upper = [jnp.maximum(a, b) for a, b in zip(upper, tops[::-1])]
        lower = [jnp.minimum(a, b) for a, b in zip(lower, bottoms[::-1])]
        return upper, lower

    def trimmed(upper, lower, total, count):
        upper_sum = (upper[0] + upper[1]) + (upper[2] + upper[3])
        lower_sum = (lower[0] + lower[1]) + (lower[2] + lower[3])
        return (total - upper_sum - lower_sum) / (count.astype(F32) - 2 * REJECT)

    edge_rows = pl.ds(al(exp * main), PAD)
    edge_spot = pl.ds(al(PAD + exp * (mine + main)), PAD)
    def smear_edge(c):
        @pl.when(has_halo)
        def _():
            for source in range(HALVES):
                halo_wait(source, c).wait_recv()
        slots = [source * visits + c * STACK + u for source in range(HALVES) for u in range(STACK)]
        stacked = jnp.concatenate([x[slot, edge_rows_of_x, :] for slot in slots], axis=0)
        both = mm(tedge[c, :, 0:REJECT * kbnd], stacked)
        smeared = both[0:REJECT * PAD] + both[REJECT * PAD:]
        return c, slots, smeared

    def pick_edge(c, slots, smeared):
        found = [cols_filter(smeared[u * PAD:(u + 1) * PAD], wide[slot]) for u, slot in enumerate(slots)]
        for n in range(columns // TILE):
            cols = slice(n * TILE, (n + 1) * TILE)
            total, count = (None, None) if c == 0 else (lists[2 * REJECT, :, cols], counts[:, cols])
            tops, bottoms, total, count = gather(
                [blocks[n] for blocks in found], [msk[slot, edge_rows, cols] for slot in slots], total, count
            )
            upper, lower = tops, bottoms
            if c > 0:
                upper, lower = merge(
                    [lists[k, :, cols] for k in range(REJECT)], [lists[REJECT + k, :, cols] for k in range(REJECT)],
                    tops, bottoms,
                )
            if c == chunks - 1:
                cpad[edge_spot, cols] = trimmed(upper, lower, total, count)
            else:
                if c > 0:
                    upper, lower = resort4(*upper), resort4(*lower)
                for k, item in enumerate(upper + lower + [total]):
                    lists[k, :, cols] = item
                counts[:, cols] = count

    held = smear_edge(0)
    for c in range(1, chunks):
        later = smear_edge(c)
        pick_edge(*held)
        held = later
    pick_edge(*held)

    def select(start):
        span = 2 * TILE

        def group(g, carry):
            rows = pl.ds(pl.multiple_of(start + (g // (columns // span)) * 8, 8), 8)
            cols = pl.ds(pl.multiple_of(lax.rem(g, columns // span) * span, span), span)
            upper, lower, total, count = None, None, None, None
            for first in range(0, HALVES * visits, REJECT):
                slots = range(first, first + REJECT)
                tops, bottoms, total, count = gather(
                    [vals[v, rows, cols] for v in slots], [msk[v, rows, cols] for v in slots], total, count
                )
                if upper is None:
                    upper, lower = tops, bottoms
                else:
                    upper, lower = merge(upper, lower, tops, bottoms)
                    if first + REJECT < HALVES * visits:
                        upper, lower = resort4(*upper), resort4(*lower)
            spot = pl.ds(pl.multiple_of(PAD + exp * mine + start + (g // (columns // span)) * 8, 8), 8)
            cpad[spot, cols] = trimmed(upper, lower, total, count)
            return carry

        lax.fori_loop(0, (PAD // 8) * (columns // span), group, 0, unroll=2)

    def share(k):
        def at(core):
            return al(PAD + jnp.where(core == 0, mine - PAD - k * PAD, mine + k * PAD))
        rows = pl.ds(at(exp), PAD)
        return remote(cpad.at[rows, :], cpad.at[rows, :], share_send.at[k], share_recv.at[k], other_core)

    def select_block(k):
        select(jnp.where(exp == 0, mine - PAD - k * PAD, k * PAD))

    edge = main // PAD
    co_halo = remote(
        cpad.at[pl.ds(al(PAD + exp * (height - PAD)), PAD), :],
        cpad.at[pl.ds(al((1 - exp) * (PAD + height)), PAD), :],
        co_send, co_recv,
        {"sky": lax.rem(sky + jnp.where(exp == 0, n_sky - 1, 1), n_sky), "exp": 1 - exp},
    )

    @pl.when(has_halo)
    def _():
        co_halo.start()
    share(edge).start()
    take_mask(1).wait_recv()
    for k in range(edge):
        select_block(k)
        share(k).start()

    def filter_rows(first, depth, rows, put_at):
        high, low = parts(cpad[pl.ds(al(first), depth), :])
        smeared = mm(tpsf[put_at:put_at + rows, 0:3 * depth], jnp.concatenate([high, low, high], axis=0))
        partial = jnp.zeros((8, TILE), F32)
        for n, block in enumerate(cols_filter(smeared, wide[psf])):
            squared = block * block
            energy[put_at:put_at + rows, n * TILE:(n + 1) * TILE] = squared
            for r in range(0, rows, 8):
                partial = partial + squared[r:r + 8]
        return partial

    steps = [(db, dx) for db in range(n_band) for dx in range(HALVES)][1:]

    def send_energy(slot, piece):
        db, dx = steps[slot]
        target = lax.rem(band + db, n_band)
        rows = (pl.ds(0, main), pl.ds(main, PAD))[piece]
        return remote(
            energy.at[rows, pl.ds(pl.multiple_of(target * width, TILE), width)],
            land.at[slot, rows, :],
            en_send.at[slot, piece], en_recv.at[slot, piece],
            {"band": target, "exp": exp if dx == 0 else 1 - exp},
        )

    @pl.when(jnp.logical_not(has_halo))
    def _():
        squares[...] = filter_rows(exp * (mine + main), kbnd, PAD, main)

    share(0).wait_recv()
    partial = filter_rows(exp * mine + (1 - exp) * PAD, kmain, main, 0)
    for slot in range(len(steps)):
        send_energy(slot, 0).start()
    for k in range(1, edge + 1):
        share(k).wait_recv()
    store_coadd = pltpu.make_async_copy(cpad.at[pl.ds(PAD, height), :], coadd_out.at[0], out_sem)
    store_coadd.start()

    @pl.when(has_halo)
    def _():
        co_halo.wait_recv()
        squares[...] = filter_rows(exp * (mine + main), kbnd, PAD, main)
    partial = partial + squares[...]
    sums[pl.ds(me, 1)] = jnp.sum(partial, axis=0, keepdims=True)[None]
    if rounds > 3:
        def relay(_, carry):
            hear()
            tell()
            return carry

        lax.fori_loop(0, rounds - 3, relay, 0)
    if rounds > 0:
        hear()

    def send_sum(step):
        return remote(sums.at[me], sums.at[me], sum_send.at[step - 1], sum_recv.at[step - 1], peer_of(step))

    def start_sum(step, carry):
        send_sum(step).start()
        return carry

    lax.fori_loop(1, n_peer, start_sum, 0, unroll=n_peer <= 16)
    for slot in range(len(steps)):
        send_energy(slot, 1).start()

    def drain(c, carry):
        @pl.when(has_after)
        def _():
            halo(0, c).wait_send()

        @pl.when(has_before)
        def _():
            halo(1, c).wait_send()
        return carry

    lax.fori_loop(0, chunks, drain, 0)
    for k in range(FAR):
        send_far(k).wait_send()
    for k in range(2):
        send_mask(k).wait_send()
    send_taps.wait_send()

    @pl.when(has_halo)
    def _():
        co_halo.wait_send()
    for k in range(edge + 1):
        share(k).wait_send()

    store_coadd.wait()
    def drain_sum(step, carry):
        send_sum(step).wait_send()
        return carry

    lax.fori_loop(1, n_peer, drain_sum, 0, unroll=n_peer <= 16)
    for slot in range(len(steps)):
        for piece in range(2):
            send_energy(slot, piece).wait_send()

    def wait_sum(step, carry):
        send_sum(step).wait_recv()
        return carry

    lax.fori_loop(1, n_peer, wait_sum, 0, unroll=n_peer <= 16)
    for slot in range(len(steps)):
        for piece in range(2):
            send_energy(slot, piece).wait_recv()


def finish(n_sky, n_band, coadd_in, energy, land, sums, coadd_out, det_out, det, sem):
    copy = pltpu.make_async_copy(coadd_in, coadd_out, sem.at[0])
    copy.start()
    band, exp = lax.axis_index("band"), lax.axis_index("exp")
    mine, columns = energy.shape
    height, width = det.shape
    main = mine - PAD
    pixels = height * n_sky * columns

    def al(value):
        return pl.multiple_of(value, PAD)

    def inverse(source):
        total = None
        for s in range(n_sky):
            for e in range(HALVES):
                term = sums[(s * n_band + source) * HALVES + e]
                total = term if total is None else total + term
        return 1.0 / (jnp.sum(total, keepdims=True) / pixels + EPSILON)

    inv = [inverse(lax.rem(band + n_band - db, n_band)) for db in range(n_band)]
    own = energy[:, pl.ds(pl.multiple_of(band * width, TILE), width)] * inv[0]
    far = land[0] * inv[0]
    for db in range(1, n_band):
        own = own + land[db * 2 - 1] * inv[db]
        far = far + land[db * 2] * inv[db]
    for core, value in ((exp, own), (1 - exp, far)):
        det[pl.ds(al(core * mine + (1 - core) * PAD), main), :] = value[0:main]
        det[pl.ds(al(core * (mine + main)), PAD), :] = value[main:]
    store = pltpu.make_async_copy(det, det_out, sem.at[1])
    store.start()
    copy.wait()
    store.wait()


def solution(mesh):
    n_sky, n_band = mesh.shape["sky"], mesh.shape["band"]

    def on_device(images, valid_mask, row_kernel, col_kernel, exp_group, zero_point, psf_row, psf_col):
        _, visits, height, columns = images.shape
        assert height == TILE and mesh.shape["exp"] == HALVES and visits % STACK == 0
        assert visits + 1 <= 16 and STACK * HALVES == REJECT
        width = columns // n_band
        mine = height // HALVES
        main = mine - PAD
        frame = mine + 2 * PAD
        chunks = visits // STACK
        slots = HALVES * visits
        n_peer = n_sky * n_band * HALVES
        n_step = n_band * HALVES - 1
        blocks = mine // PAD
        hbm, anywhere = (pl.BlockSpec(memory_space=space) for space in (pltpu.HBM, pl.ANY))
        dma = pltpu.SemaphoreType.DMA
        vmem = pl.BlockSpec(memory_space=pltpu.VMEM)
        found = pl.pallas_call(
            functools.partial(kernel, n_sky, n_band),
            out_shape=(
                pltpu.VMEM((1, height, columns), F32),
                pltpu.VMEM((mine, columns), F32),
                pltpu.VMEM((n_step, mine, width), F32),
                pltpu.VMEM((n_peer, 1, TILE), F32),
            ),
            in_specs=[hbm] * 8,
            out_specs=(anywhere, vmem, vmem, vmem),
            scratch_shapes=[
                pltpu.VMEM((visits, 1, TAPS), F32),
                pltpu.VMEM((visits, 1, TAPS), F32),
                pltpu.VMEM((1, TAPS), F32),
                pltpu.VMEM((1, TAPS), F32),
                pltpu.SMEM(exp_group.shape, jnp.int32),
                pltpu.SMEM(zero_point.shape, F32),
                pltpu.VMEM((slots, frame, columns), BF),
                pltpu.VMEM((slots, mine, columns), jnp.int32),
                pltpu.VMEM((2, 2, 16, 2 * TILE), F32),
                pltpu.VMEM((slots, 2 * main, TILE), BF),
                pltpu.VMEM((chunks, 2 * REJECT * PAD, 2 * TILE), BF),
                pltpu.VMEM((mine, 2 * TILE), BF),
                pltpu.VMEM((slots + 1, 2 * TILE, 2 * TILE), BF),
                pltpu.VMEM((slots, mine, columns), F32),
                pltpu.VMEM((2 * REJECT + 1, PAD, columns), F32),
                pltpu.VMEM((PAD, columns), jnp.int32),
                pltpu.VMEM((8, TILE), F32),
                pltpu.VMEM((height + 2 * PAD, columns), F32),
                dma((6,)), dma, dma, dma, dma, dma((FAR,)), dma((FAR,)), dma((2,)), dma((2,)),
                dma((2, chunks)), dma((2, chunks)), dma((blocks,)), dma((blocks,)), dma, dma,
                dma((n_peer - 1,)), dma((n_peer - 1,)), dma((n_step, 2)), dma((n_step, 2)), dma,
                pltpu.SemaphoreType.REGULAR((2,)),
            ],
            compiler_params=pltpu.CompilerParams(
                collective_id=0, has_side_effects=True, vmem_limit_bytes=48 << 20
            ),
        )(*(
            pltpu.with_memory_space_constraint(array, pltpu.HBM)
            for array in (
                images, valid_mask, jnp.swapaxes(row_kernel, 0, 1), jnp.swapaxes(col_kernel, 0, 1),
                psf_row, psf_col, exp_group, zero_point,
            )
        ))
        return pl.pallas_call(
            functools.partial(finish, n_sky, n_band),
            out_shape=(
                jax.ShapeDtypeStruct((1, height, columns), F32),
                jax.ShapeDtypeStruct((height, width), F32),
            ),
            in_specs=[anywhere, vmem, vmem, vmem],
            out_specs=(anywhere, anywhere),
            scratch_shapes=[pltpu.VMEM((height, width), F32), dma((2,))],
            compiler_params=pltpu.CompilerParams(vmem_limit_bytes=1 << 20),
        )(*found)

    placed = (
        P("band", "exp", ("patch", "sky"), None),
        P("band", "exp", ("patch", "sky"), None),
        P("band", "exp", None),
        P("band", "exp", None),
        P("band", "exp"),
        P("band", None),
        P("band", None),
        P("band", None),
    )
    return jax.shard_map(
        on_device,
        mesh=mesh,
        in_specs=placed,
        out_specs=(P("band", ("patch", "sky"), None), P(("patch", "sky"), "band")),
        check_vma=False,
    )
```

```python
import functools

import jax
import jax.numpy as jnp
from jax import lax
from jax.experimental import pallas as pl
from jax.experimental.pallas import tpu as pltpu
from jax.sharding import PartitionSpec as P

MESH = pl.DeviceIdType.MESH
HALF = 15
REJECT = 4
TAPS = 31
SENTINEL = 1e30
EPSILON = 1e-05
PAD = 16
TILE = 128
HALVES = 2
STACK = 2
AHEAD = 2
FAR = 2
BF = jnp.bfloat16
F32 = jnp.float32


def parts(value):
    high = value.astype(BF)
    return high, (value - high.astype(F32)).astype(BF)


def mm(a, b):
    return jnp.dot(a, b, preferred_element_type=F32)


def cols_filter(value, matrix):
    rows, columns = value.shape
    blocks = columns // TILE
    high, low = parts(value)
    zero = jnp.zeros((rows, TILE), BF)
    cut = [slice(n * TILE, (n + 1) * TILE) for n in range(blocks)]
    left = [jnp.concatenate([high[:, at], high[:, at]], axis=1) for at in cut]
    left += [jnp.concatenate([low[:, at], zero], axis=1) for at in cut]
    spread = mm(jnp.concatenate(left, axis=0), matrix)
    spread = [spread[n * rows:(n + 1) * rows] + spread[(blocks + n) * rows:(blocks + n + 1) * rows] for n in range(blocks)]
    joined = [spread[0][:, 0:TILE]]
    for n in range(1, blocks):
        joined.append(spread[n][:, 0:TILE] + spread[n - 1][:, TILE:])
    joined.append(spread[-1][:, TILE:])
    joined = [pltpu.roll(part, TILE // 2, 1) for part in joined]
    first = lax.broadcasted_iota(jnp.int32, (rows, TILE), 1) < TILE // 2
    return [jnp.where(first, joined[n], joined[n + 1]) for n in range(blocks)]


def swap(a, b):
    return jnp.minimum(a, b), jnp.maximum(a, b)


def sort4(a, b, c, d):
    a, b = swap(a, b)
    c, d = swap(c, d)
    a, c = swap(a, c)
    b, d = swap(b, d)
    b, c = swap(b, c)
    return [a, b, c, d]


def resort4(a, b, c, d):
    a, c = swap(a, c)
    b, d = swap(b, d)
    a, b = swap(a, b)
    c, d = swap(c, d)
    return [a, b, c, d]


def kernel(
    n_sky, n_band,
    img, mask, rk_in, ck_in, pr_in, pc_in, eg_in, zp_in,
    coadd_out, energy, land, sums,
    rk, ck, pr, pc, eg, zp, x, msk, taps, trow, tedge, tpsf, wide, vals, lists, counts, squares, cpad,
    arg_sem, img_sem, mask_sem, tap_send, tap_recv, far_send, far_recv, fmask_send, fmask_recv,
    halo_send, halo_recv, share_send, share_recv, co_send, co_recv, sum_send, sum_recv, en_send, en_recv, out_sem, token,
):
    visits, height, columns = img.shape[1:]
    mine = height // HALVES
    main = mine - PAD
    frame = mine + 2 * PAD
    kmain, kbnd = main + 2 * PAD, 3 * PAD
    width = columns // n_band
    chunks = visits // STACK
    sky, band, exp = lax.axis_index("sky"), lax.axis_index("band"), lax.axis_index("exp")
    has_before, has_after = sky > 0, sky < n_sky - 1
    has_halo = jnp.where(exp == 0, sky, n_sky - 1 - sky) > 0
    n_peer = n_sky * n_band * HALVES
    me = (sky * n_band + band) * HALVES + exp

    def peer_of(step):
        peer = lax.rem(me + step, n_peer)
        chip = peer // HALVES
        return {"sky": chip // n_band, "band": lax.rem(chip, n_band), "exp": lax.rem(peer, HALVES)}

    other_core = {"exp": 1 - exp}

    def remote(source, target, send, recv, device):
        return pltpu.make_async_remote_copy(
            src_ref=source, dst_ref=target, send_sem=send, recv_sem=recv, device_id=device, device_id_type=MESH,
        )

    def al(value):
        return pl.multiple_of(value, PAD)

    barrier = pltpu.get_barrier_semaphore()

    def beside(side):
        return lax.rem(sky + (1, n_sky - 1)[side], n_sky)

    exists = (has_after, has_before)
    for side in range(2):
        @pl.when(exists[side])
        def _():
            for core in range(HALVES):
                pl.semaphore_signal(barrier, inc=1, device_id={"sky": beside(side), "exp": core}, device_id_type=MESH)
    pl.semaphore_signal(barrier, inc=1, device_id=other_core, device_id_type=MESH)
    for db in range(1, n_band):
        for core in range(HALVES):
            pl.semaphore_signal(
                barrier, inc=1, device_id={"band": lax.rem(band + db, n_band), "exp": core}, device_id_type=MESH
            )

    small = [
        pltpu.make_async_copy(source, target, arg_sem.at[k])
        for k, (source, target) in enumerate(
            ((eg_in, eg), (zp_in, zp), (ck_in, ck), (pc_in, pc), (rk_in, rk), (pr_in, pr))
        )
    ]
    for copy in small:
        copy.start()

    load_img = pltpu.make_async_copy(
        img.at[0, :, pl.ds(al(exp * (mine - PAD)), kmain), :],
        x.at[pl.ds(0, visits), pl.ds(al((1 - exp) * PAD), kmain), :], img_sem,
    )
    load_img.start()
    load_mask = pltpu.make_async_copy(
        mask.at[0, :, pl.ds(al(exp * mine), mine), :], msk.at[pl.ds(0, visits)], mask_sem
    )
    load_mask.start()
    taps[0] = jnp.zeros(taps.shape[1:], F32)
    for copy in small:
        copy.wait()
    for v in range(visits):
        taps[0, 0, v:v + 1, 0:TAPS] = rk[v]
    taps[0, 0, visits:visits + 1, 0:TAPS] = pr[...]
    for v in range(visits):
        taps[0, 1, v:v + 1, 0:TAPS] = ck[v] * zp[0, eg[0, v]]
    taps[0, 1, visits:visits + 1, 0:TAPS] = pc[...]
    at_row = lax.broadcasted_iota(jnp.int32, (TILE, TILE), 0)
    at_col = lax.broadcasted_iota(jnp.int32, (TILE, TILE), 1)
    flip = (at_col == TILE // 2 + HALF - at_row).astype(F32)
    taps[0, 1, :, 0:TILE] = jnp.dot(taps[0, 1, :, 0:TILE], flip, preferred_element_type=F32, precision=lax.Precision.HIGHEST)
    greeted = sum(jnp.where(there, HALVES, 0) for there in exists)
    pl.semaphore_wait(barrier, greeted + 1 + HALVES * (n_band - 1))

    rounds = n_sky - 1

    def tell():
        for side in range(2):
            @pl.when(exists[side])
            def _():
                pl.semaphore_signal(token.at[side], inc=1, device_id={"sky": beside(side)}, device_id_type=MESH)

    def hear():
        for side in range(2):
            @pl.when(exists[1 - side])
            def _():
                pl.semaphore_wait(token.at[side], 1)

    def halo(side, c):
        start, land_at = ((height - PAD, 0), (0, PAD + mine))[side]
        slot = jnp.where(exp == side, 0, visits) + c * STACK
        return remote(
            img.at[0, pl.ds(c * STACK, STACK), pl.ds(start, PAD), :],
            x.at[pl.ds(slot, STACK), pl.ds(land_at, PAD), :],
            halo_send.at[side, c], halo_recv.at[jnp.where(exp == side, 0, 1), c],
            {"sky": beside(side), "exp": side},
        )

    def start_halo(c, carry):
        @pl.when(has_after)
        def _():
            halo(0, c).start()

        @pl.when(has_before)
        def _():
            halo(1, c).start()
        return carry

    lax.fori_loop(0, chunks, start_halo, 0)

    def send_far(k):
        some = visits // FAR
        return remote(
            img.at[0, pl.ds(k * some, some), pl.ds(al((1 - exp) * (mine - PAD)), kmain), :],
            x.at[pl.ds(visits + k * some, some), pl.ds(al(exp * PAD), kmain), :],
            far_send.at[k], far_recv.at[k], other_core,
        )

    def take_far(k):
        some = visits // FAR
        piece = x.at[pl.ds(visits + k * some, some), pl.ds(al((1 - exp) * PAD), kmain), :]
        return remote(piece, piece, far_send.at[k], far_recv.at[k], other_core)

    for k in range(FAR):
        send_far(k).start()
    def send_mask(k):
        far = 1 - exp
        start, rows = ((far * main, PAD), ((1 - far) * PAD, main))[k]
        return remote(
            mask.at[0, :, pl.ds(al(far * mine + start), rows), :],
            msk.at[pl.ds(visits, visits), pl.ds(al(start), rows), :],
            fmask_send.at[k], fmask_recv.at[k], other_core,
        )

    def take_mask(k):
        start, rows = ((exp * main, PAD), ((1 - exp) * PAD, main))[k]
        piece = msk.at[pl.ds(visits, visits), pl.ds(al(start), rows), :]
        return remote(piece, piece, fmask_send.at[k], fmask_recv.at[k], other_core)

    send_mask(0).start()
    tell()

    send_taps = remote(taps.at[0], taps.at[1], tap_send, tap_recv, other_core)
    send_taps.start()
    send_mask(1).start()

    @pl.when(jnp.logical_not(has_halo))
    def _():
        x[:, pl.ds(al(exp * (PAD + mine)), PAD), :] = jnp.zeros((HALVES * visits, PAD, columns), BF)
        cpad[pl.ds(al(exp * (PAD + height)), PAD), :] = jnp.zeros((PAD, columns), F32)

    upward = (at_col > at_row).astype(F32).astype(BF)

    def slanted(origin, v, rows, lanes, shift):
        line = jnp.broadcast_to(taps[origin, 0, v:v + 1, 0:lanes], (rows, lanes))
        return pltpu.roll(line, shift, 1, stride=1, stride_axis=0)

    def build_wide(origin, v, slot):
        line = jnp.broadcast_to(taps[origin, 1, v:v + 1, 0:TILE], (TILE, TILE))
        line = pltpu.roll(line, 0, 1, stride=1, stride_axis=0)
        for n, part in enumerate(parts(line)):
            here = part * upward
            wide[slot, n * TILE:(n + 1) * TILE, 0:TILE] = here
            wide[slot, n * TILE:(n + 1) * TILE, TILE:] = part - here

    def build(origin, v):
        slot = origin * visits + v
        for n, part in enumerate(parts(slanted(origin, v, main, TILE, 1))):
            trow[slot, n * main:(n + 1) * main, :] = part
        group, j = v // STACK, origin * STACK + v % STACK
        for n, part in enumerate(parts(slanted(origin, v, PAD, 2 * TILE, j * kbnd + 1))):
            tedge[group, (n * REJECT + j) * PAD:(n * REJECT + j + 1) * PAD, :] = part
        build_wide(origin, v, slot)

    def smear(slot):
        both = mm(trow[slot, :, 0:kmain], x[slot, pl.ds(al((1 - exp) * PAD), kmain), :])
        return both[0:main] + both[main:]

    def put(slot, start, rows, value):
        for n, block in enumerate(cols_filter(value, wide[slot])):
            vals[slot, pl.ds(al(start), rows), n * TILE:(n + 1) * TILE] = block

    def convolve(origin):
        waiting = []
        for v in range(visits):
            if origin and v % (visits // FAR) == 0:
                take_far(v // (visits // FAR)).wait_recv()
            build(origin, v)
            slot = origin * visits + v
            waiting.append((slot, smear(slot)))
            if len(waiting) > AHEAD:
                done, value = waiting.pop(0)
                put(done, (1 - exp) * PAD, main, value)
        for done, value in waiting:
            put(done, (1 - exp) * PAD, main, value)

    load_img.wait()
    convolve(0)
    if rounds > 1:
        hear()
        tell()
    send_taps.wait_recv()
    convolve(1)
    if rounds > 2:
        hear()
        tell()

    psf = HALVES * visits
    build_wide(0, visits, psf)
    for rows, depth, at in ((main, kmain, 0), (PAD, kbnd, main)):
        pieces = [parts(slanted(0, visits, rows, 2 * TILE, j * depth + 1))[int(j == 2)] for j in range(3)]
        tpsf[at:at + rows, :] = pieces[0] + pieces[1] + pieces[2]

    edge_rows_of_x = pl.ds(al(exp * main), kbnd)

    def halo_wait(source, c):
        land_at = al(exp * (PAD + mine))
        piece = x.at[pl.ds(source * visits + c * STACK, STACK), pl.ds(land_at, PAD), :]
        return remote(piece, piece, halo_send.at[0, c], halo_recv.at[source, c], other_core)

    load_mask.wait()
    take_mask(0).wait_recv()

    def gather(values, masks, total, count):
        tops, bottoms = [], []
        for value, used in zip(values, masks):
            live = used == 1
            tops.append(jnp.where(live, value, -SENTINEL))
            bottoms.append(jnp.where(live, value, SENTINEL))
            kept = jnp.where(live, value, 0.0)
            total = kept if total is None else total + kept
            count = used if count is None else count + used
        return sort4(*tops), sort4(*bottoms), total, count

    def merge(upper, lower, tops, bottoms):
        upper = [jnp.maximum(a, b) for a, b in zip(upper, tops[::-1])]
        lower = [jnp.minimum(a, b) for a, b in zip(lower, bottoms[::-1])]
        return upper, lower

    def trimmed(upper, lower, total, count):
        upper_sum = (upper[0] + upper[1]) + (upper[2] + upper[3])
        lower_sum = (lower[0] + lower[1]) + (lower[2] + lower[3])
        return (total - upper_sum - lower_sum) / (count.astype(F32) - 2 * REJECT)

    edge_rows = pl.ds(al(exp * main), PAD)
    edge_spot = pl.ds(al(PAD + exp * (mine + main)), PAD)
    def smear_edge(c):
        @pl.when(has_halo)
        def _():
            for source in range(HALVES):
                halo_wait(source, c).wait_recv()
        slots = [source * visits + c * STACK + u for source in range(HALVES) for u in range(STACK)]
        stacked = jnp.concatenate([x[slot, edge_rows_of_x, :] for slot in slots], axis=0)
        both = mm(tedge[c, :, 0:REJECT * kbnd], stacked)
        smeared = both[0:REJECT * PAD] + both[REJECT * PAD:]
        return c, slots, smeared

    def pick_edge(c, slots, smeared):
        found = [cols_filter(smeared[u * PAD:(u + 1) * PAD], wide[slot]) for u, slot in enumerate(slots)]
        for n in range(columns // TILE):
            cols = slice(n * TILE, (n + 1) * TILE)
            total, count = (None, None) if c == 0 else (lists[2 * REJECT, :, cols], counts[:, cols])
            tops, bottoms, total, count = gather(
                [blocks[n] for blocks in found], [msk[slot, edge_rows, cols] for slot in slots], total, count
            )
            upper, lower = tops, bottoms
            if c > 0:
                upper, lower = merge(
                    [lists[k, :, cols] for k in range(REJECT)], [lists[REJECT + k, :, cols] for k in range(REJECT)],
                    tops, bottoms,
                )
            if c == chunks - 1:
                cpad[edge_spot, cols] = trimmed(upper, lower, total, count)
            else:
                if c > 0:
                    upper, lower = resort4(*upper), resort4(*lower)
                for k, item in enumerate(upper + lower + [total]):
                    lists[k, :, cols] = item
                counts[:, cols] = count

    held = smear_edge(0)
    for c in range(1, chunks):
        later = smear_edge(c)
        pick_edge(*held)
        held = later
    pick_edge(*held)

    def select(start):
        span = 2 * TILE

        def group(g, carry):
            rows = pl.ds(pl.multiple_of(start + (g // (columns // span)) * 8, 8), 8)
            cols = pl.ds(pl.multiple_of(lax.rem(g, columns // span) * span, span), span)
            upper, lower, total, count = None, None, None, None
            for first in range(0, HALVES * visits, REJECT):
                slots = range(first, first + REJECT)
                tops, bottoms, total, count = gather(
                    [vals[v, rows, cols] for v in slots], [msk[v, rows, cols] for v in slots], total, count
                )
                if upper is None:
                    upper, lower = tops, bottoms
                else:
                    upper, lower = merge(upper, lower, tops, bottoms)
                    if first + REJECT < HALVES * visits:
                        upper, lower = resort4(*upper), resort4(*lower)
            spot = pl.ds(pl.multiple_of(PAD + exp * mine + start + (g // (columns // span)) * 8, 8), 8)
            cpad[spot, cols] = trimmed(upper, lower, total, count)
            return carry

        lax.fori_loop(0, (PAD // 8) * (columns // span), group, 0, unroll=2)

    def share(k):
        def at(core):
            return al(PAD + jnp.where(core == 0, mine - PAD - k * PAD, mine + k * PAD))
        rows = pl.ds(at(exp), PAD)
        return remote(cpad.at[rows, :], cpad.at[rows, :], share_send.at[k], share_recv.at[k], other_core)

    def select_block(k):
        select(jnp.where(exp == 0, mine - PAD - k * PAD, k * PAD))

    edge = main // PAD
    co_halo = remote(
        cpad.at[pl.ds(al(PAD + exp * (height - PAD)), PAD), :],
        cpad.at[pl.ds(al((1 - exp) * (PAD + height)), PAD), :],
        co_send, co_recv,
        {"sky": lax.rem(sky + jnp.where(exp == 0, n_sky - 1, 1), n_sky), "exp": 1 - exp},
    )

    @pl.when(has_halo)
    def _():
        co_halo.start()
    share(edge).start()
    take_mask(1).wait_recv()
    for k in range(edge):
        select_block(k)
        share(k).start()

    def filter_rows(first, depth, rows, put_at):
        high, low = parts(cpad[pl.ds(al(first), depth), :])
        smeared = mm(tpsf[put_at:put_at + rows, 0:3 * depth], jnp.concatenate([high, low, high], axis=0))
        partial = jnp.zeros((8, TILE), F32)
        for n, block in enumerate(cols_filter(smeared, wide[psf])):
            squared = block * block
            energy[put_at:put_at + rows, n * TILE:(n + 1) * TILE] = squared
            for r in range(0, rows, 8):
                partial = partial + squared[r:r + 8]
        return partial

    steps = [(db, dx) for db in range(n_band) for dx in range(HALVES)][1:]

    def send_energy(slot, piece):
        db, dx = steps[slot]
        target = lax.rem(band + db, n_band)
        rows = (pl.ds(0, main), pl.ds(main, PAD))[piece]
        return remote(
            energy.at[rows, pl.ds(pl.multiple_of(target * width, TILE), width)],
            land.at[slot, rows, :],
            en_send.at[slot, piece], en_recv.at[slot, piece],
            {"band": target, "exp": exp if dx == 0 else 1 - exp},
        )

    @pl.when(jnp.logical_not(has_halo))
    def _():
        squares[...] = filter_rows(exp * (mine + main), kbnd, PAD, main)

    share(0).wait_recv()
    partial = filter_rows(exp * mine + (1 - exp) * PAD, kmain, main, 0)
    for slot in range(len(steps)):
        send_energy(slot, 0).start()
    for k in range(1, edge + 1):
        share(k).wait_recv()
    store_coadd = pltpu.make_async_copy(cpad.at[pl.ds(PAD, height), :], coadd_out.at[0], out_sem)
    store_coadd.start()
    if rounds > 3:
        def relay(_, carry):
            hear()
            tell()
            return carry

        lax.fori_loop(0, rounds - 3, relay, 0)
    if rounds > 0:
        hear()


    @pl.when(has_halo)
    def _():
        co_halo.wait_recv()
        squares[...] = filter_rows(exp * (mine + main), kbnd, PAD, main)
    partial = partial + squares[...]
    sums[pl.ds(me, 1)] = jnp.sum(partial, axis=0, keepdims=True)[None]
    def send_sum(step):
        return remote(sums.at[me], sums.at[me], sum_send.at[step - 1], sum_recv.at[step - 1], peer_of(step))

    def start_sum(step, carry):
        send_sum(step).start()
        return carry

    lax.fori_loop(1, n_peer, start_sum, 0, unroll=n_peer <= 16)
    for slot in range(len(steps)):
        send_energy(slot, 1).start()

    def drain(c, carry):
        @pl.when(has_after)
        def _():
            halo(0, c).wait_send()

        @pl.when(has_before)
        def _():
            halo(1, c).wait_send()
        return carry

    lax.fori_loop(0, chunks, drain, 0)
    for k in range(FAR):
        send_far(k).wait_send()
    for k in range(2):
        send_mask(k).wait_send()
    send_taps.wait_send()

    @pl.when(has_halo)
    def _():
        co_halo.wait_send()
    for k in range(edge + 1):
        share(k).wait_send()

    store_coadd.wait()
    def drain_sum(step, carry):
        send_sum(step).wait_send()
        return carry

    lax.fori_loop(1, n_peer, drain_sum, 0, unroll=n_peer <= 16)
    for slot in range(len(steps)):
        for piece in range(2):
            send_energy(slot, piece).wait_send()

    def wait_sum(step, carry):
        send_sum(step).wait_recv()
        return carry

    lax.fori_loop(1, n_peer, wait_sum, 0, unroll=n_peer <= 16)
    for slot in range(len(steps)):
        for piece in range(2):
            send_energy(slot, piece).wait_recv()


def finish(n_sky, n_band, coadd_in, energy, land, sums, coadd_out, det_out, det, sem):
    copy = pltpu.make_async_copy(coadd_in, coadd_out, sem.at[0])
    copy.start()
    band, exp = lax.axis_index("band"), lax.axis_index("exp")
    mine, columns = energy.shape
    height, width = det.shape
    main = mine - PAD
    pixels = height * n_sky * columns

    def al(value):
        return pl.multiple_of(value, PAD)

    def inverse(source):
        total = None
        for s in range(n_sky):
            for e in range(HALVES):
                term = sums[(s * n_band + source) * HALVES + e]
                total = term if total is None else total + term
        return 1.0 / (jnp.sum(total, keepdims=True) / pixels + EPSILON)

    inv = [inverse(lax.rem(band + n_band - db, n_band)) for db in range(n_band)]
    own = energy[:, pl.ds(pl.multiple_of(band * width, TILE), width)] * inv[0]
    far = land[0] * inv[0]
    for db in range(1, n_band):
        own = own + land[db * 2 - 1] * inv[db]
        far = far + land[db * 2] * inv[db]
    for core, value in ((exp, own), (1 - exp, far)):
        det[pl.ds(al(core * mine + (1 - core) * PAD), main), :] = value[0:main]
        det[pl.ds(al(core * (mine + main)), PAD), :] = value[main:]
    store = pltpu.make_async_copy(det, det_out, sem.at[1])
    store.start()
    copy.wait()
    store.wait()


def solution(mesh):
    n_sky, n_band = mesh.shape["sky"], mesh.shape["band"]

    def on_device(images, valid_mask, row_kernel, col_kernel, exp_group, zero_point, psf_row, psf_col):
        _, visits, height, columns = images.shape
        assert height == TILE and mesh.shape["exp"] == HALVES and visits % STACK == 0
        assert visits + 1 <= 16 and STACK * HALVES == REJECT
        width = columns // n_band
        mine = height // HALVES
        main = mine - PAD
        frame = mine + 2 * PAD
        chunks = visits // STACK
        slots = HALVES * visits
        n_peer = n_sky * n_band * HALVES
        n_step = n_band * HALVES - 1
        blocks = mine // PAD
        hbm, anywhere = (pl.BlockSpec(memory_space=space) for space in (pltpu.HBM, pl.ANY))
        dma = pltpu.SemaphoreType.DMA
        vmem = pl.BlockSpec(memory_space=pltpu.VMEM)
        found = pl.pallas_call(
            functools.partial(kernel, n_sky, n_band),
            out_shape=(
                pltpu.VMEM((1, height, columns), F32),
                pltpu.VMEM((mine, columns), F32),
                pltpu.VMEM((n_step, mine, width), F32),
                pltpu.VMEM((n_peer, 1, TILE), F32),
            ),
            in_specs=[hbm] * 8,
            out_specs=(anywhere, vmem, vmem, vmem),
            scratch_shapes=[
                pltpu.VMEM((visits, 1, TAPS), F32),
                pltpu.VMEM((visits, 1, TAPS), F32),
                pltpu.VMEM((1, TAPS), F32),
                pltpu.VMEM((1, TAPS), F32),
                pltpu.SMEM(exp_group.shape, jnp.int32),
                pltpu.SMEM(zero_point.shape, F32),
                pltpu.VMEM((slots, frame, columns), BF),
                pltpu.VMEM((slots, mine, columns), jnp.int32),
                pltpu.VMEM((2, 2, 16, 2 * TILE), F32),
                pltpu.VMEM((slots, 2 * main, TILE), BF),
                pltpu.VMEM((chunks, 2 * REJECT * PAD, 2 * TILE), BF),
                pltpu.VMEM((mine, 2 * TILE), BF),
                pltpu.VMEM((slots + 1, 2 * TILE, 2 * TILE), BF),
                pltpu.VMEM((slots, mine, columns), F32),
                pltpu.VMEM((2 * REJECT + 1, PAD, columns), F32),
                pltpu.VMEM((PAD, columns), jnp.int32),
                pltpu.VMEM((8, TILE), F32),
                pltpu.VMEM((height + 2 * PAD, columns), F32),
                dma((6,)), dma, dma, dma, dma, dma((FAR,)), dma((FAR,)), dma((2,)), dma((2,)),
                dma((2, chunks)), dma((2, chunks)), dma((blocks,)), dma((blocks,)), dma, dma,
                dma((n_peer - 1,)), dma((n_peer - 1,)), dma((n_step, 2)), dma((n_step, 2)), dma,
                pltpu.SemaphoreType.REGULAR((2,)),
            ],
            compiler_params=pltpu.CompilerParams(
                collective_id=0, has_side_effects=True, vmem_limit_bytes=48 << 20
            ),
        )(*(
            pltpu.with_memory_space_constraint(array, pltpu.HBM)
            for array in (
                images, valid_mask, jnp.swapaxes(row_kernel, 0, 1), jnp.swapaxes(col_kernel, 0, 1),
                psf_row, psf_col, exp_group, zero_point,
            )
        ))
        return pl.pallas_call(
            functools.partial(finish, n_sky, n_band),
            out_shape=(
                jax.ShapeDtypeStruct((1, height, columns), F32),
                jax.ShapeDtypeStruct((height, width), F32),
            ),
            in_specs=[anywhere, vmem, vmem, vmem],
            out_specs=(anywhere, anywhere),
            scratch_shapes=[pltpu.VMEM((height, width), F32), dma((2,))],
            compiler_params=pltpu.CompilerParams(vmem_limit_bytes=1 << 20),
        )(*found)

    placed = (
        P("band", "exp", ("patch", "sky"), None),
        P("band", "exp", ("patch", "sky"), None),
        P("band", "exp", None),
        P("band", "exp", None),
        P("band", "exp"),
        P("band", None),
        P("band", None),
        P("band", None),
    )
    return jax.shard_map(
        on_device,
        mesh=mesh,
        in_specs=placed,
        out_specs=(P("band", ("patch", "sky"), None), P(("patch", "sky"), "band")),
        check_vma=False,
    )
```

```python
import functools

import jax
import jax.numpy as jnp
from jax import lax
from jax.experimental import pallas as pl
from jax.experimental.pallas import tpu as pltpu
from jax.sharding import PartitionSpec as P

MESH = pl.DeviceIdType.MESH
HALF = 15
REJECT = 4
TAPS = 31
SENTINEL = 1e30
EPSILON = 1e-05
PAD = 16
TILE = 128
HALVES = 2
STACK = 2
AHEAD = 2
FAR = 2
BF = jnp.bfloat16
F32 = jnp.float32


def parts(value):
    high = value.astype(BF)
    return high, (value - high.astype(F32)).astype(BF)


def mm(a, b):
    return jnp.dot(a, b, preferred_element_type=F32)


def cols_filter(value, matrix):
    rows, columns = value.shape
    blocks = columns // TILE
    high, low = parts(value)
    zero = jnp.zeros((rows, TILE), BF)
    cut = [slice(n * TILE, (n + 1) * TILE) for n in range(blocks)]
    left = [jnp.concatenate([high[:, at], high[:, at]], axis=1) for at in cut]
    left += [jnp.concatenate([low[:, at], zero], axis=1) for at in cut]
    spread = mm(jnp.concatenate(left, axis=0), matrix)
    spread = [spread[n * rows:(n + 1) * rows] + spread[(blocks + n) * rows:(blocks + n + 1) * rows] for n in range(blocks)]
    joined = [spread[0][:, 0:TILE]]
    for n in range(1, blocks):
        joined.append(spread[n][:, 0:TILE] + spread[n - 1][:, TILE:])
    joined.append(spread[-1][:, TILE:])
    joined = [pltpu.roll(part, TILE // 2, 1) for part in joined]
    first = lax.broadcasted_iota(jnp.int32, (rows, TILE), 1) < TILE // 2
    return [jnp.where(first, joined[n], joined[n + 1]) for n in range(blocks)]


def swap(a, b):
    return jnp.minimum(a, b), jnp.maximum(a, b)


def sort4(a, b, c, d):
    a, b = swap(a, b)
    c, d = swap(c, d)
    a, c = swap(a, c)
    b, d = swap(b, d)
    b, c = swap(b, c)
    return [a, b, c, d]


def resort4(a, b, c, d):
    a, c = swap(a, c)
    b, d = swap(b, d)
    a, b = swap(a, b)
    c, d = swap(c, d)
    return [a, b, c, d]


def kernel(
    n_sky, n_band,
    img, mask, rk_in, ck_in, pr_in, pc_in, eg_in, zp_in,
    coadd_out, energy, land, sums,
    rk, ck, pr, pc, eg, zp, x, msk, taps, trow, tedge, tpsf, wide, vals, lists, counts, squares, cpad,
    arg_sem, img_sem, mask_sem, tap_send, tap_recv, far_send, far_recv, fmask_send, fmask_recv,
    halo_send, halo_recv, share_send, share_recv, co_send, co_recv, sum_send, sum_recv, en_send, en_recv, out_sem, token,
):
    visits, height, columns = img.shape[1:]
    mine = height // HALVES
    main = mine - PAD
    frame = mine + 2 * PAD
    kmain, kbnd = main + 2 * PAD, 3 * PAD
    width = columns // n_band
    chunks = visits // STACK
    sky, band, exp = lax.axis_index("sky"), lax.axis_index("band"), lax.axis_index("exp")
    has_before, has_after = sky > 0, sky < n_sky - 1
    has_halo = jnp.where(exp == 0, sky, n_sky - 1 - sky) > 0
    n_peer = n_sky * n_band * HALVES
    me = (sky * n_band + band) * HALVES + exp

    def peer_of(step):
        peer = lax.rem(me + step, n_peer)
        chip = peer // HALVES
        return {"sky": chip // n_band, "band": lax.rem(chip, n_band), "exp": lax.rem(peer, HALVES)}

    other_core = {"exp": 1 - exp}

    def remote(source, target, send, recv, device):
        return pltpu.make_async_remote_copy(
            src_ref=source, dst_ref=target, send_sem=send, recv_sem=recv, device_id=device, device_id_type=MESH,
        )

    def al(value):
        return pl.multiple_of(value, PAD)

    barrier = pltpu.get_barrier_semaphore()

    def beside(side):
        return lax.rem(sky + (1, n_sky - 1)[side], n_sky)

    exists = (has_after, has_before)
    for side in range(2):
        @pl.when(exists[side])
        def _():
            for core in range(HALVES):
                pl.semaphore_signal(barrier, inc=1, device_id={"sky": beside(side), "exp": core}, device_id_type=MESH)
    pl.semaphore_signal(barrier, inc=1, device_id=other_core, device_id_type=MESH)
    for db in range(1, n_band):
        for core in range(HALVES):
            pl.semaphore_signal(
                barrier, inc=1, device_id={"band": lax.rem(band + db, n_band), "exp": core}, device_id_type=MESH
            )

    small = [
        pltpu.make_async_copy(source, target, arg_sem.at[k])
        for k, (source, target) in enumerate(
            ((eg_in, eg), (zp_in, zp), (ck_in, ck), (pc_in, pc), (rk_in, rk), (pr_in, pr))
        )
    ]
    for copy in small:
        copy.start()

    load_img = pltpu.make_async_copy(
        img.at[0, :, pl.ds(al(exp * (mine - PAD)), kmain), :],
        x.at[pl.ds(0, visits), pl.ds(al((1 - exp) * PAD), kmain), :], img_sem,
    )
    load_img.start()
    load_mask = pltpu.make_async_copy(
        mask.at[0, :, pl.ds(al(exp * mine), mine), :], msk.at[pl.ds(0, visits)], mask_sem
    )
    load_mask.start()
    taps[0] = jnp.zeros(taps.shape[1:], F32)
    for copy in small:
        copy.wait()
    for v in range(visits):
        taps[0, 0, v:v + 1, 0:TAPS] = rk[v]
    taps[0, 0, visits:visits + 1, 0:TAPS] = pr[...]
    for v in range(visits):
        taps[0, 1, v:v + 1, 0:TAPS] = ck[v] * zp[0, eg[0, v]]
    taps[0, 1, visits:visits + 1, 0:TAPS] = pc[...]
    at_row = lax.broadcasted_iota(jnp.int32, (TILE, TILE), 0)
    at_col = lax.broadcasted_iota(jnp.int32, (TILE, TILE), 1)
    flip = (at_col == TILE // 2 + HALF - at_row).astype(F32)
    taps[0, 1, :, 0:TILE] = jnp.dot(taps[0, 1, :, 0:TILE], flip, preferred_element_type=F32, precision=lax.Precision.HIGHEST)
    greeted = sum(jnp.where(there, HALVES, 0) for there in exists)
    pl.semaphore_wait(barrier, greeted + 1 + HALVES * (n_band - 1))

    rounds = n_sky - 1

    def tell():
        for side in range(2):
            @pl.when(exists[side])
            def _():
                pl.semaphore_signal(token.at[side], inc=1, device_id={"sky": beside(side)}, device_id_type=MESH)

    def hear():
        for side in range(2):
            @pl.when(exists[1 - side])
            def _():
                pl.semaphore_wait(token.at[side], 1)

    def halo(side, c):
        start, land_at = ((height - PAD, 0), (0, PAD + mine))[side]
        slot = jnp.where(exp == side, 0, visits) + c * STACK
        return remote(
            img.at[0, pl.ds(c * STACK, STACK), pl.ds(start, PAD), :],
            x.at[pl.ds(slot, STACK), pl.ds(land_at, PAD), :],
            halo_send.at[side, c], halo_recv.at[jnp.where(exp == side, 0, 1), c],
            {"sky": beside(side), "exp": side},
        )

    def start_halo(c, carry):
        @pl.when(has_after)
        def _():
            halo(0, c).start()

        @pl.when(has_before)
        def _():
            halo(1, c).start()
        return carry

    lax.fori_loop(0, chunks, start_halo, 0)

    def send_far(k):
        some = visits // FAR
        return remote(
            img.at[0, pl.ds(k * some, some), pl.ds(al((1 - exp) * (mine - PAD)), kmain), :],
            x.at[pl.ds(visits + k * some, some), pl.ds(al(exp * PAD), kmain), :],
            far_send.at[k], far_recv.at[k], other_core,
        )

    def take_far(k):
        some = visits // FAR
        piece = x.at[pl.ds(visits + k * some, some), pl.ds(al((1 - exp) * PAD), kmain), :]
        return remote(piece, piece, far_send.at[k], far_recv.at[k], other_core)

    for k in range(FAR):
        send_far(k).start()
    def send_mask(k):
        far = 1 - exp
        start, rows = ((far * main, PAD), ((1 - far) * PAD, main))[k]
        return remote(
            mask.at[0, :, pl.ds(al(far * mine + start), rows), :],
            msk.at[pl.ds(visits, visits), pl.ds(al(start), rows), :],
            fmask_send.at[k], fmask_recv.at[k], other_core,
        )

    def take_mask(k):
        start, rows = ((exp * main, PAD), ((1 - exp) * PAD, main))[k]
        piece = msk.at[pl.ds(visits, visits), pl.ds(al(start), rows), :]
        return remote(piece, piece, fmask_send.at[k], fmask_recv.at[k], other_core)

    send_mask(0).start()
    tell()

    send_taps = remote(taps.at[0], taps.at[1], tap_send, tap_recv, other_core)
    send_taps.start()
    send_mask(1).start()

    @pl.when(jnp.logical_not(has_halo))
    def _():
        x[:, pl.ds(al(exp * (PAD + mine)), PAD), :] = jnp.zeros((HALVES * visits, PAD, columns), BF)
        cpad[pl.ds(al(exp * (PAD + height)), PAD), :] = jnp.zeros((PAD, columns), F32)

    upward = (at_col > at_row).astype(F32).astype(BF)

    def slanted(origin, v, rows, lanes, shift):
        line = jnp.broadcast_to(taps[origin, 0, v:v + 1, 0:lanes], (rows, lanes))
        return pltpu.roll(line, shift, 1, stride=1, stride_axis=0)

    def build_wide(origin, v, slot):
        line = jnp.broadcast_to(taps[origin, 1, v:v + 1, 0:TILE], (TILE, TILE))
        line = pltpu.roll(line, 0, 1, stride=1, stride_axis=0)
        for n, part in enumerate(parts(line)):
            here = part * upward
            wide[slot, n * TILE:(n + 1) * TILE, 0:TILE] = here
            wide[slot, n * TILE:(n + 1) * TILE, TILE:] = part - here

    def build(origin, v):
        slot = origin * visits + v
        for n, part in enumerate(parts(slanted(origin, v, main, TILE, 1))):
            trow[slot, n * main:(n + 1) * main, :] = part
        group, j = v // STACK, origin * STACK + v % STACK
        for n, part in enumerate(parts(slanted(origin, v, PAD, 2 * TILE, j * kbnd + 1))):
            tedge[group, (n * REJECT + j) * PAD:(n * REJECT + j + 1) * PAD, :] = part
        build_wide(origin, v, slot)

    def smear(slot):
        both = mm(trow[slot, :, 0:kmain], x[slot, pl.ds(al((1 - exp) * PAD), kmain), :])
        return both[0:main] + both[main:]

    def put(slot, start, rows, value):
        for n, block in enumerate(cols_filter(value, wide[slot])):
            vals[slot, pl.ds(al(start), rows), n * TILE:(n + 1) * TILE] = block

    def convolve(origin):
        waiting = []
        for v in range(visits):
            if origin and v % (visits // FAR) == 0:
                take_far(v // (visits // FAR)).wait_recv()
            build(origin, v)
            slot = origin * visits + v
            waiting.append((slot, smear(slot)))
            if len(waiting) > AHEAD:
                done, value = waiting.pop(0)
                put(done, (1 - exp) * PAD, main, value)
        for done, value in waiting:
            put(done, (1 - exp) * PAD, main, value)

    load_img.wait()
    convolve(0)
    if rounds > 1:
        hear()
        tell()
    send_taps.wait_recv()
    convolve(1)
    if rounds > 2:
        hear()
        tell()

    psf = HALVES * visits
    build_wide(0, visits, psf)
    for rows, depth, at in ((main, kmain, 0), (PAD, kbnd, main)):
        pieces = [parts(slanted(0, visits, rows, 2 * TILE, j * depth + 1))[int(j == 2)] for j in range(3)]
        tpsf[at:at + rows, :] = pieces[0] + pieces[1] + pieces[2]

    edge_rows_of_x = pl.ds(al(exp * main), kbnd)

    def halo_wait(source, c):
        land_at = al(exp * (PAD + mine))
        piece = x.at[pl.ds(source * visits + c * STACK, STACK), pl.ds(land_at, PAD), :]
        return remote(piece, piece, halo_send.at[0, c], halo_recv.at[source, c], other_core)

    load_mask.wait()
    take_mask(0).wait_recv()

    def gather(values, masks, total, count):
        tops, bottoms = [], []
        for value, used in zip(values, masks):
            live = used == 1
            tops.append(jnp.where(live, value, -SENTINEL))
            bottoms.append(jnp.where(live, value, SENTINEL))
            kept = jnp.where(live, value, 0.0)
            total = kept if total is None else total + kept
            count = used if count is None else count + used
        return sort4(*tops), sort4(*bottoms), total, count

    def merge(upper, lower, tops, bottoms):
        upper = [jnp.maximum(a, b) for a, b in zip(upper, tops[::-1])]
        lower = [jnp.minimum(a, b) for a, b in zip(lower, bottoms[::-1])]
        return upper, lower

    def trimmed(upper, lower, total, count):
        upper_sum = (upper[0] + upper[1]) + (upper[2] + upper[3])
        lower_sum = (lower[0] + lower[1]) + (lower[2] + lower[3])
        return (total - upper_sum - lower_sum) / (count.astype(F32) - 2 * REJECT)

    edge_rows = pl.ds(al(exp * main), PAD)
    edge_spot = pl.ds(al(PAD + exp * (mine + main)), PAD)
    def smear_edge(c):
        @pl.when(has_halo)
        def _():
            for source in range(HALVES):
                halo_wait(source, c).wait_recv()
        slots = [source * visits + c * STACK + u for source in range(HALVES) for u in range(STACK)]
        stacked = jnp.concatenate([x[slot, edge_rows_of_x, :] for slot in slots], axis=0)
        both = mm(tedge[c, :, 0:REJECT * kbnd], stacked)
        smeared = both[0:REJECT * PAD] + both[REJECT * PAD:]
        return c, slots, smeared

    def pick_edge(c, slots, smeared):
        found = [cols_filter(smeared[u * PAD:(u + 1) * PAD], wide[slot]) for u, slot in enumerate(slots)]
        for n in range(columns // TILE):
            cols = slice(n * TILE, (n + 1) * TILE)
            total, count = (None, None) if c == 0 else (lists[2 * REJECT, :, cols], counts[:, cols])
            tops, bottoms, total, count = gather(
                [blocks[n] for blocks in found], [msk[slot, edge_rows, cols] for slot in slots], total, count
            )
            upper, lower = tops, bottoms
            if c > 0:
                upper, lower = merge(
                    [lists[k, :, cols] for k in range(REJECT)], [lists[REJECT + k, :, cols] for k in range(REJECT)],
                    tops, bottoms,
                )
            if c == chunks - 1:
                cpad[edge_spot, cols] = trimmed(upper, lower, total, count)
            else:
                if c > 0:
                    upper, lower = resort4(*upper), resort4(*lower)
                for k, item in enumerate(upper + lower + [total]):
                    lists[k, :, cols] = item
                counts[:, cols] = count

    held = smear_edge(0)
    for c in range(1, chunks):
        later = smear_edge(c)
        pick_edge(*held)
        held = later
    pick_edge(*held)

    def select(start):
        span = 2 * TILE

        def group(g, carry):
            rows = pl.ds(pl.multiple_of(start + (g // (columns // span)) * 8, 8), 8)
            cols = pl.ds(pl.multiple_of(lax.rem(g, columns // span) * span, span), span)
            upper, lower, total, count = None, None, None, None
            for first in range(0, HALVES * visits, REJECT):
                slots = range(first, first + REJECT)
                tops, bottoms, total, count = gather(
                    [vals[v, rows, cols] for v in slots], [msk[v, rows, cols] for v in slots], total, count
                )
                if upper is None:
                    upper, lower = tops, bottoms
                else:
                    upper, lower = merge(upper, lower, tops, bottoms)
                    if first + REJECT < HALVES * visits:
                        upper, lower = resort4(*upper), resort4(*lower)
            spot = pl.ds(pl.multiple_of(PAD + exp * mine + start + (g // (columns // span)) * 8, 8), 8)
            cpad[spot, cols] = trimmed(upper, lower, total, count)
            return carry

        lax.fori_loop(0, (PAD // 8) * (columns // span), group, 0, unroll=2)

    def share(k):
        def at(core):
            return al(PAD + jnp.where(core == 0, mine - PAD - k * PAD, mine + k * PAD))
        rows = pl.ds(at(exp), PAD)
        return remote(cpad.at[rows, :], cpad.at[rows, :], share_send.at[k], share_recv.at[k], other_core)

    def select_block(k):
        select(jnp.where(exp == 0, mine - PAD - k * PAD, k * PAD))

    edge = main // PAD
    co_halo = remote(
        cpad.at[pl.ds(al(PAD + exp * (height - PAD)), PAD), :],
        cpad.at[pl.ds(al((1 - exp) * (PAD + height)), PAD), :],
        co_send, co_recv,
        {"sky": lax.rem(sky + jnp.where(exp == 0, n_sky - 1, 1), n_sky), "exp": 1 - exp},
    )

    @pl.when(has_halo)
    def _():
        co_halo.start()
    share(edge).start()
    take_mask(1).wait_recv()
    for k in range(edge):
        select_block(k)
        share(k).start()

    def filter_rows(first, depth, rows, put_at):
        high, low = parts(cpad[pl.ds(al(first), depth), :])
        smeared = mm(tpsf[put_at:put_at + rows, 0:3 * depth], jnp.concatenate([high, low, high], axis=0))
        partial = jnp.zeros((8, TILE), F32)
        for n, block in enumerate(cols_filter(smeared, wide[psf])):
            squared = block * block
            energy[put_at:put_at + rows, n * TILE:(n + 1) * TILE] = squared
            for r in range(0, rows, 8):
                partial = partial + squared[r:r + 8]
        return partial

    steps = [(db, dx) for db in range(n_band) for dx in range(HALVES)][1:]

    def send_energy(slot, piece):
        db, dx = steps[slot]
        target = lax.rem(band + db, n_band)
        rows = (pl.ds(0, main), pl.ds(main, PAD))[piece]
        return remote(
            energy.at[rows, pl.ds(pl.multiple_of(target * width, TILE), width)],
            land.at[slot, rows, :],
            en_send.at[slot, piece], en_recv.at[slot, piece],
            {"band": target, "exp": exp if dx == 0 else 1 - exp},
        )

    @pl.when(jnp.logical_not(has_halo))
    def _():
        squares[...] = filter_rows(exp * (mine + main), kbnd, PAD, main)

    share(0).wait_recv()
    partial = filter_rows(exp * mine + (1 - exp) * PAD, kmain, main, 0)
    for slot in range(len(steps)):
        send_energy(slot, 0).start()
    for k in range(1, edge + 1):
        share(k).wait_recv()
    store_coadd = pltpu.make_async_copy(cpad.at[pl.ds(PAD, height), :], coadd_out.at[0], out_sem)
    store_coadd.start()

    @pl.when(has_halo)
    def _():
        co_halo.wait_recv()
        squares[...] = filter_rows(exp * (mine + main), kbnd, PAD, main)
    partial = partial + squares[...]
    sums[pl.ds(me, 1)] = jnp.sum(partial, axis=0, keepdims=True)[None]
    if rounds > 3:
        def relay(_, carry):
            hear()
            tell()
            return carry

        lax.fori_loop(0, rounds - 3, relay, 0)
    if rounds > 0:
        hear()

    def send_sum(step):
        return remote(sums.at[me], sums.at[me], sum_send.at[step - 1], sum_recv.at[step - 1], peer_of(step))

    def start_sum(step, carry):
        send_sum(step).start()
        return carry

    lax.fori_loop(1, n_peer, start_sum, 0, unroll=n_peer <= 16)
    for slot in range(len(steps)):
        send_energy(slot, 1).start()

    def drain(c, carry):
        @pl.when(has_after)
        def _():
            halo(0, c).wait_send()

        @pl.when(has_before)
        def _():
            halo(1, c).wait_send()
        return carry

    lax.fori_loop(0, chunks, drain, 0)
    for k in range(FAR):
        send_far(k).wait_send()
    for k in range(2):
        send_mask(k).wait_send()
    send_taps.wait_send()

    @pl.when(has_halo)
    def _():
        co_halo.wait_send()
    for k in range(edge + 1):
        share(k).wait_send()

    store_coadd.wait()
    def drain_sum(step, carry):
        send_sum(step).wait_send()
        return carry

    lax.fori_loop(1, n_peer, drain_sum, 0, unroll=n_peer <= 16)
    for slot in range(len(steps)):
        for piece in range(2):
            send_energy(slot, piece).wait_send()

    def wait_sum(step, carry):
        send_sum(step).wait_recv()
        return carry

    lax.fori_loop(1, n_peer, wait_sum, 0, unroll=n_peer <= 16)
    for slot in range(len(steps)):
        for piece in range(2):
            send_energy(slot, piece).wait_recv()


def finish(n_sky, n_band, coadd_in, energy, land, sums, coadd_out, det_out, det, sem):
    copy = pltpu.make_async_copy(coadd_in, coadd_out, sem.at[0])
    copy.start()
    band, exp = lax.axis_index("band"), lax.axis_index("exp")
    mine, columns = energy.shape
    height, width = det.shape
    main = mine - PAD
    pixels = height * n_sky * columns

    def al(value):
        return pl.multiple_of(value, PAD)

    def inverse(source):
        total = None
        for s in range(n_sky):
            for e in range(HALVES):
                term = sums[(s * n_band + source) * HALVES + e]
                total = term if total is None else total + term
        return 1.0 / (jnp.sum(total, keepdims=True) / pixels + EPSILON)

    inv = [inverse(lax.rem(band + n_band - db, n_band)) for db in range(n_band)]
    own = energy[:, pl.ds(pl.multiple_of(band * width, TILE), width)] * inv[0]
    far = land[0] * inv[0]
    for db in range(1, n_band):
        own = own + land[db * 2 - 1] * inv[db]
        far = far + land[db * 2] * inv[db]
    stores = []
    for core, value in ((exp, own), (1 - exp, far)):
        det[pl.ds(al(core * mine + (1 - core) * PAD), main), :] = value[0:main]
        det[pl.ds(al(core * (mine + main)), PAD), :] = value[main:]
        rows = pl.ds(al(core * mine), mine)
        stores.append(pltpu.make_async_copy(det.at[rows, :], det_out.at[rows, :], sem.at[len(stores) + 1]))
        stores[-1].start()
    copy.wait()
    for store in stores:
        store.wait()


def solution(mesh):
    n_sky, n_band = mesh.shape["sky"], mesh.shape["band"]

    def on_device(images, valid_mask, row_kernel, col_kernel, exp_group, zero_point, psf_row, psf_col):
        _, visits, height, columns = images.shape
        assert height == TILE and mesh.shape["exp"] == HALVES and visits % STACK == 0
        assert visits + 1 <= 16 and STACK * HALVES == REJECT
        width = columns // n_band
        mine = height // HALVES
        main = mine - PAD
        frame = mine + 2 * PAD
        chunks = visits // STACK
        slots = HALVES * visits
        n_peer = n_sky * n_band * HALVES
        n_step = n_band * HALVES - 1
        blocks = mine // PAD
        hbm, anywhere = (pl.BlockSpec(memory_space=space) for space in (pltpu.HBM, pl.ANY))
        dma = pltpu.SemaphoreType.DMA
        vmem = pl.BlockSpec(memory_space=pltpu.VMEM)
        found = pl.pallas_call(
            functools.partial(kernel, n_sky, n_band),
            out_shape=(
                pltpu.VMEM((1, height, columns), F32),
                pltpu.VMEM((mine, columns), F32),
                pltpu.VMEM((n_step, mine, width), F32),
                pltpu.VMEM((n_peer, 1, TILE), F32),
            ),
            in_specs=[hbm] * 8,
            out_specs=(anywhere, vmem, vmem, vmem),
            scratch_shapes=[
                pltpu.VMEM((visits, 1, TAPS), F32),
                pltpu.VMEM((visits, 1, TAPS), F32),
                pltpu.VMEM((1, TAPS), F32),
                pltpu.VMEM((1, TAPS), F32),
                pltpu.SMEM(exp_group.shape, jnp.int32),
                pltpu.SMEM(zero_point.shape, F32),
                pltpu.VMEM((slots, frame, columns), BF),
                pltpu.VMEM((slots, mine, columns), jnp.int32),
                pltpu.VMEM((2, 2, 16, 2 * TILE), F32),
                pltpu.VMEM((slots, 2 * main, TILE), BF),
                pltpu.VMEM((chunks, 2 * REJECT * PAD, 2 * TILE), BF),
                pltpu.VMEM((mine, 2 * TILE), BF),
                pltpu.VMEM((slots + 1, 2 * TILE, 2 * TILE), BF),
                pltpu.VMEM((slots, mine, columns), F32),
                pltpu.VMEM((2 * REJECT + 1, PAD, columns), F32),
                pltpu.VMEM((PAD, columns), jnp.int32),
                pltpu.VMEM((8, TILE), F32),
                pltpu.VMEM((height + 2 * PAD, columns), F32),
                dma((6,)), dma, dma, dma, dma, dma((FAR,)), dma((FAR,)), dma((2,)), dma((2,)),
                dma((2, chunks)), dma((2, chunks)), dma((blocks,)), dma((blocks,)), dma, dma,
                dma((n_peer - 1,)), dma((n_peer - 1,)), dma((n_step, 2)), dma((n_step, 2)), dma,
                pltpu.SemaphoreType.REGULAR((2,)),
            ],
            compiler_params=pltpu.CompilerParams(
                collective_id=0, has_side_effects=True, vmem_limit_bytes=48 << 20
            ),
        )(*(
            pltpu.with_memory_space_constraint(array, pltpu.HBM)
            for array in (
                images, valid_mask, jnp.swapaxes(row_kernel, 0, 1), jnp.swapaxes(col_kernel, 0, 1),
                psf_row, psf_col, exp_group, zero_point,
            )
        ))
        return pl.pallas_call(
            functools.partial(finish, n_sky, n_band),
            out_shape=(
                jax.ShapeDtypeStruct((1, height, columns), F32),
                jax.ShapeDtypeStruct((height, width), F32),
            ),
            in_specs=[anywhere, vmem, vmem, vmem],
            out_specs=(anywhere, anywhere),
            scratch_shapes=[pltpu.VMEM((height, width), F32), dma((3,))],
            compiler_params=pltpu.CompilerParams(vmem_limit_bytes=1 << 20),
        )(*found)

    placed = (
        P("band", "exp", ("patch", "sky"), None),
        P("band", "exp", ("patch", "sky"), None),
        P("band", "exp", None),
        P("band", "exp", None),
        P("band", "exp"),
        P("band", None),
        P("band", None),
        P("band", None),
    )
    return jax.shard_map(
        on_device,
        mesh=mesh,
        in_specs=placed,
        out_specs=(P("band", ("patch", "sky"), None), P(("patch", "sky"), "band")),
        check_vma=False,
    )
```
